512 devices in a mesh: occ: 16 (over z, y_lo), vir: 32 (over x, y_hi, core).
Axes of the slice: x: 4, y: 8 (y_hi: 4, y_lo: 2; y = y_hi * 2 + y_lo), z: 8, core: 2. Of those that a mesh axis runs over, the one named last changes fastest.
Arguments:
- amplitudes: float32 [32, 16, 256, 256], P('occ', None, 'vir'), may hold values from -6 to 6
- integrals: float32 [16, 256, 32, 256], P(None, 'occ', None, 'vir'), may hold values from -0.25 to 0.25
- tile_mask: int32 [32, 16, 4, 4], P('occ'), may hold values 0 or 1
- tile_irrep: int32 [36], replicated, may hold values from 0 to 7
Outputs:
- residual: float32 [32, 256, 32, 256], P('occ', 'vir')
The draws below stay inside these ranges and needn't reach their ends.
All inputs are finite; a program needn't handle non-finite values. No bound on the sum of `tile_mask` on one device may be relied on, other than what follows from the above.
Results may differ from the reference program's by a relative error of at most 0.00007.
Values sent between devices are 32-bit elements; how exact they have to be, the bound alone decides.
A program may use at most 64 MiB of HBM per device.

```python
import jax
import jax.numpy as jnp
from jax import lax

NO = 32
V = 256
TILE = 64
KW = 16
NVT = 4


def place_ends(result, key, low, high):
    extent = result.shape
    spot = [jax.random.randint(jax.random.fold_in(key, axis), (), 0, extent[axis]) for axis in range(len(extent))]
    result = result.at[tuple(spot)].set(low)
    longest = extent.index(max(extent))
    spot[longest] = (spot[longest] + 1) % extent[longest]
    return result.at[tuple(spot)].set(high)


def levels(rng, extent, split, low, top_value):
    def one(axis_at, shards_of):
        steps = jax.random.uniform(jax.random.fold_in(jax.random.fold_in(rng, 6), axis_at), (shards_of,), jnp.float32, low / len(split), top_value / len(split))
        return jnp.repeat(jnp.exp(steps), extent[axis_at] // shards_of).reshape((-1,) + (1,) * (len(extent) - axis_at - 1))

    gain = one(*split[0])
    for cut in split[1:]:
        gain = gain * one(*cut)
    return gain


def centred(stream_key, extent, scale, reach, split=(), kind=jnp.bfloat16):
    result = scale * jax.random.normal(stream_key, extent, jnp.float32)
    if split:
        result = result * levels(stream_key, extent, split, -0.22, 0.18)
    return jnp.clip(result, -reach, reach).astype(kind)


def setup_inputs(seed: int = 0) -> dict:
    splits = jax.random.split(jax.random.key(seed), 5)
    amplitudes = centred(splits[0], (NO, KW, V, V), 1.0, 6.0, ((0, 16), (2, 32)), jnp.float32)
    integrals = centred(splits[1], (KW, V, NO, V), (KW * V // 8) ** -0.5, 0.25, ((1, 16), (3, 32)), jnp.float32)
    tile_mask = place_ends((jax.random.randint(splits[2], (NO, KW, NVT, NVT), 0, 2) < 1).astype(jnp.int32), jax.random.fold_in(splits[2], 1), 0, 1)
    tile_irrep = place_ends(jax.random.randint(splits[3], (NO + NVT,), 0, 8), jax.random.fold_in(splits[3], 1), 0, 7).astype(jnp.int32)
    return dict(amplitudes=amplitudes, integrals=integrals, tile_mask=tile_mask, tile_irrep=tile_irrep)


def reference(amplitudes, integrals, tile_mask, tile_irrep):
    occ_label = tile_irrep[:NO]
    vir_label = jnp.repeat(tile_irrep[NO:], TILE)
    parity = jnp.bitwise_xor(jnp.bitwise_xor(occ_label[:KW, None, None, None], vir_label[None, :, None, None]), jnp.bitwise_xor(occ_label[None, None, :, None], vir_label[None, None, None, :]))
    wsym = integrals * (parity == 0).astype(integrals.dtype)
    kept = jnp.repeat(jnp.repeat(tile_mask, TILE, 2), TILE, 3).astype(amplitudes.dtype)
    tkept = amplitudes * kept
    left = tkept.transpose(0, 3, 1, 2).reshape(NO * V, KW * V)
    right = wsym.reshape(KW * V, NO * V)
    cycle = jnp.dot(left, right, precision=lax.Precision.HIGHEST, preferred_element_type=jnp.float32)
    cycle = cycle.reshape(NO, V, NO, V).transpose(0, 3, 2, 1)
    return cycle - cycle.transpose(2, 1, 0, 3)
```

```python
import jax
import jax.numpy as jnp
from jax import lax
from jax.experimental import pallas as pl
from jax.experimental.pallas import tpu as pltpu
from jax.sharding import PartitionSpec as P

NO = 32
V = 256
TILE = 64
KW = 16
MESH = pl.DeviceIdType.MESH
F32 = jnp.float32
BF16 = jnp.bfloat16


def split(value):
    high = value.astype(BF16)
    return high, (value - high.astype(F32)).astype(BF16)


def kernel(amp_ref, int_ref, mask_ref, irrep_ref, out_ref, amp_all, int_all, acc, cyc, mirror, send_sem, recv_sem, pass_send, pass_recv):
    occ, vir = lax.axis_index("occ"), lax.axis_index("vir")
    z, yl = occ // 2, occ % 2
    x, yh, core = vir // 8, (vir // 2) % 4, vir % 2

    def occ_at(dz, flip):
        return ((z + dz + 8) % 8) * 2 + (yl + flip) % 2

    def vir_at(dx, dy, flip):
        return (((x + dx + 4) % 4) * 4 + (yh + dy + 4) % 4) * 2 + (core + flip) % 2

    barrier = pltpu.get_barrier_semaphore()
    for step in range(1, 16):
        pl.semaphore_signal(barrier, inc=1, device_id=((occ + step) % 16, vir), device_id_type=MESH)
    for dx, dy, flip in ((1, 0, 0), (-1, 0, 0), (0, 1, 0), (0, -1, 0), (0, 0, 1)):
        pl.semaphore_signal(barrier, inc=1, device_id=(occ, vir_at(dx, dy, flip)), device_id_type=MESH)

    spread = (lax.broadcasted_iota(jnp.int32, (4, V), 1) // TILE == lax.broadcasted_iota(jnp.int32, (4, V), 0)).astype(F32)
    for i in range(2):
        kept = lax.dot_general(
            mask_ref[i, vir // 8].astype(F32), spread, (((0,), (0,)), ((), ())), preferred_element_type=F32
        )
        amp_all[i, vir] = amp_ref[i] * kept[:, None, :]

    lane = lax.broadcasted_iota(jnp.int32, (NO, V), 1) // 16
    row = lax.broadcasted_iota(jnp.int32, (NO, V), 0)
    label = jnp.full((NO, V), irrep_ref[NO + occ // 4] ^ irrep_ref[NO + vir // 8], jnp.int32)
    lanes = jnp.zeros((NO, V), jnp.int32)
    rows = jnp.zeros((NO, V), jnp.int32)
    for k in range(KW):
        lanes = jnp.where(lane == k, irrep_ref[k], lanes)
    for j in range(NO):
        rows = jnp.where(row == j, irrep_ref[j], rows)
    symmetry = ((label ^ lanes ^ rows) == 0).astype(F32)
    for b in range(8):
        int_all[occ, b * NO : (b + 1) * NO, :] = int_ref[pl.ds(b, V, stride=8), :].T * symmetry

    pl.semaphore_wait(barrier, 20)

    count = [0]
    sent = []

    def move(source, to, landing):
        slot = count[0]
        count[0] += 1
        copy = pltpu.make_async_remote_copy(
            src_ref=source, dst_ref=source, send_sem=send_sem.at[slot], recv_sem=recv_sem.at[slot], device_id=to, device_id_type=MESH
        )
        copy.start()
        sent.append(copy)
        arrival = pltpu.make_async_remote_copy(
            src_ref=landing, dst_ref=landing, send_sem=send_sem.at[slot], recv_sem=recv_sem.at[slot], device_id=to, device_id_type=MESH
        )
        return arrival.wait_recv

    arrivals = []
    x_wait = {}
    y_wait = {}
    z_wait = {}

    def block(i, dx, dy, flip=0):
        return amp_all.at[i, vir_at(dx, dy, flip)]

    def half(i, dx, dy, upper):
        return amp_all.at[i, vir_at(dx, dy, 0), pl.ds(8 * upper, 8)]

    right, left = (occ, vir_at(1, 0, 0)), (occ, vir_at(-1, 0, 0))
    up, down = (occ, vir_at(0, 1, 0)), (occ, vir_at(0, -1, 0))
    sibling = (occ, vir_at(0, 0, 1))

    def share(i, dx, dy):
        arrivals.append(move(block(i, dx, dy), sibling, block(i, dx, dy, 1)))

    def x_start(i, dy):
        x_wait[i, dy] = (
            move(block(i, 0, dy), right, block(i, -1, dy)),
            move(block(i, 0, dy), left, block(i, 1, dy)),
        )
        share(i, 0, dy)

    def x_forward(i, dy):
        first, second = x_wait[i, dy]
        first()
        one = move(half(i, -1, dy, 0), right, half(i, 2, dy, 0))
        share(i, -1, dy)
        second()
        two = move(half(i, 1, dy, 1), left, half(i, 2, dy, 1))
        share(i, 1, dy)
        x_wait[i, dy] = (one, two)

    def x_end(i, dy):
        one, two = x_wait[i, dy]
        one()
        two()
        share(i, 2, dy)

    def y_start(i):
        y_wait[i] = [move(block(i, 0, 0), up, block(i, 0, -1)), move(block(i, 0, 0), down, block(i, 0, 1))]

    def y_forward(i):
        first, second = y_wait[i]
        first()
        one = move(half(i, 0, -1, 0), up, half(i, 0, 2, 0))
        x_start(i, -1)
        second()
        two = move(half(i, 0, 1, 1), down, half(i, 0, 2, 1))
        x_start(i, 1)
        y_wait[i] = [one, two]

    def y_end(i):
        one, two = y_wait[i]
        one()
        two()
        x_start(i, 2)

    above, below = (occ_at(1, 0), vir), (occ_at(-1, 0), vir)

    def z_start(flip):
        z_wait[flip] = (
            move(int_all.at[occ_at(0, flip)], above, int_all.at[occ_at(-1, flip)]),
            move(int_all.at[occ_at(0, flip)], below, int_all.at[occ_at(1, flip)]),
        )

    def z_forward(flip, hop):
        first, second = z_wait[flip]
        first()
        if hop < 3:
            one = move(int_all.at[occ_at(-hop, flip)], above, int_all.at[occ_at(-hop - 1, flip)])
        else:
            one = move(int_all.at[occ_at(-3, flip), pl.ds(0, 128)], above, int_all.at[occ_at(4, flip), pl.ds(0, 128)])
        second()
        if hop < 3:
            two = move(int_all.at[occ_at(hop, flip)], below, int_all.at[occ_at(hop + 1, flip)])
        else:
            two = move(int_all.at[occ_at(3, flip), pl.ds(128, 128)], below, int_all.at[occ_at(4, flip), pl.ds(128, 128)])
        z_wait[flip] = (one, two)

    def z_end(flip):
        one, two = z_wait[flip]
        one()
        two()

    pair_wait = move(int_all.at[occ], (occ_at(0, 1), vir), int_all.at[occ_at(0, 1)])
    z_start(0)
    y_start(0)
    x_start(0, 0)
    y_start(1)
    x_start(1, 0)
    x_forward(0, 0)
    pair_wait()
    z_start(1)
    z_forward(0, 1)
    y_forward(0)
    x_forward(1, 0)
    y_forward(1)
    z_forward(1, 1)
    x_forward(0, -1)
    x_forward(0, 1)
    y_end(0)
    z_forward(0, 2)
    x_end(0, 0)
    x_end(1, 0)
    y_end(1)
    x_forward(1, -1)
    z_forward(1, 2)
    x_forward(1, 1)
    x_forward(0, 2)
    z_forward(0, 3)
    x_forward(1, 2)
    x_end(0, -1)
    x_end(0, 1)
    x_end(1, -1)
    x_end(1, 1)
    z_forward(1, 3)
    x_end(0, 2)
    x_end(1, 2)
    z_end(0)
    z_end(1)
    for wait in arrivals:
        wait()

    acc[...] = jnp.zeros_like(acc)

    def contract(o, carry):
        int_high, int_low = split(int_all[o])
        left_side = jnp.concatenate([int_high, int_high, int_low], axis=1)
        for i in range(2):
            piece = jnp.concatenate([amp_all[i, 2 * o][:, None], amp_all[i, 2 * o + 1][:, None]], axis=1).reshape(V, V)
            amp_high, amp_low = split(piece)
            right_side = jnp.concatenate([amp_high, amp_low, amp_high], axis=0)
            acc[i] += jnp.dot(left_side, right_side, preferred_element_type=F32)
        return carry

    lax.fori_loop(0, 16, contract, 0)

    for i in range(2):
        for b in range(8):
            for h in range(2):
                cyc[i, h, pl.ds(b, NO, stride=8), :] = acc[i, b * NO : (b + 1) * NO, h * 128 : (h + 1) * 128]
    passed = []
    for i in range(2):
        for step in range(1, 16):
            slot = i * 15 + step - 1
            to, origin = (occ + step) % 16, (occ + 16 - step) % 16
            copy = pltpu.make_async_remote_copy(
                src_ref=cyc.at[i, :, pl.ds(16 * to, 16)],
                dst_ref=mirror.at[:, pl.ds((2 * occ + i) * 16, 16)],
                send_sem=pass_send.at[slot],
                recv_sem=pass_recv.at[slot],
                device_id=(to, vir),
                device_id_type=MESH,
            )
            copy.start()
            landing = mirror.at[:, pl.ds((2 * origin + i) * 16, 16)]
            passed.append(
                (
                    copy,
                    pltpu.make_async_remote_copy(
                        src_ref=landing,
                        dst_ref=landing,
                        send_sem=pass_send.at[slot],
                        recv_sem=pass_recv.at[slot],
                        device_id=(to, vir),
                        device_id_type=MESH,
                    ),
                )
            )
        mirror[:, pl.ds((2 * occ + i) * 16, 16), :] = cyc[i, :, pl.ds(16 * occ, 16), :]
    for copy, arrival in passed:
        arrival.wait_recv()
    for i in range(2):
        for b in range(8):
            for h in range(2):
                out_ref[i, b, :, h * 128 : (h + 1) * 128] = (
                    acc[i, b * NO : (b + 1) * NO, h * 128 : (h + 1) * 128] - mirror[h, pl.ds(i * 8 + b, NO, stride=16), :]
                )
    for copy in sent:
        copy.wait_send()
    for copy, arrival in passed:
        copy.wait_send()


MOVES = 2 * (4 + 16 + 16) + 17


def body(amplitudes, integrals, tile_mask, tile_irrep):
    flat_int = integrals.transpose(0, 1, 3, 2).reshape(KW * 16 * 8, NO)
    mask = tile_mask.transpose(0, 2, 3, 1)
    vmem = pl.BlockSpec(memory_space=pltpu.VMEM)
    return pl.pallas_call(
        kernel,
        out_shape=jax.ShapeDtypeStruct((2, 8, NO, V), F32),
        in_specs=[vmem, vmem, vmem, pl.BlockSpec(memory_space=pltpu.SMEM)],
        out_specs=vmem,
        scratch_shapes=[
            pltpu.VMEM((2, 32, KW, 8, V), F32),
            pltpu.VMEM((16, V, V), F32),
            pltpu.VMEM((2, V, V), F32),
            pltpu.VMEM((2, 2, V, 128), F32),
            pltpu.VMEM((2, 2 * V, 128), F32),
            pltpu.SemaphoreType.DMA((MOVES,)),
            pltpu.SemaphoreType.DMA((MOVES,)),
            pltpu.SemaphoreType.DMA((30,)),
            pltpu.SemaphoreType.DMA((30,)),
        ],
        compiler_params=pltpu.CompilerParams(collective_id=0, has_side_effects=True, vmem_limit_bytes=48 << 20),
    )(amplitudes, flat_int, mask, tile_irrep)


def solution(mesh):
    return jax.shard_map(
        body,
        mesh=mesh,
        in_specs=(
            P("occ", None, "vir", None),
            P(None, "occ", None, "vir"),
            P("occ", None, None, None),
            P(),
        ),
        out_specs=P("occ", "vir", None, None),
        check_vma=False,
    )
```

```python
import jax
import jax.numpy as jnp
from jax import lax
from jax.experimental import pallas as pl
from jax.experimental.pallas import tpu as pltpu
from jax.sharding import PartitionSpec as P

NO = 32
V = 256
TILE = 64
KW = 16
DEPTH = 16
FAR_FIRST = (8, 7, 9, 6, 10, 5, 11, 4, 12, 3, 13, 2, 14, 1, 15)
MESH = pl.DeviceIdType.MESH
F32 = jnp.float32
BF16 = jnp.bfloat16


def split(value):
    high = value.astype(BF16)
    return high, (value - high.astype(F32)).astype(BF16)


def dense_kernel(amp_ref, int_ref, mask_ref, irrep_ref, out_ref, amp_all, int_all, acc, cyc, mirror, send_sem, recv_sem, pass_send, pass_recv):
    occ, vir = lax.axis_index("occ"), lax.axis_index("vir")
    z, yl = occ // 2, occ % 2
    x, yh, core = vir // 8, (vir // 2) % 4, vir % 2

    def occ_at(dz, flip):
        return ((z + dz + 8) % 8) * 2 + (yl + flip) % 2

    def vir_at(dx, dy, flip):
        return (((x + dx + 4) % 4) * 4 + (yh + dy + 4) % 4) * 2 + (core + flip) % 2

    barrier = pltpu.get_barrier_semaphore()
    for step in range(1, 16):
        pl.semaphore_signal(barrier, inc=1, device_id=((occ + step) % 16, vir), device_id_type=MESH)
    for dx, dy, flip in ((1, 0, 0), (-1, 0, 0), (0, 1, 0), (0, -1, 0), (0, 0, 1)):
        pl.semaphore_signal(barrier, inc=1, device_id=(occ, vir_at(dx, dy, flip)), device_id_type=MESH)

    spread = (lax.broadcasted_iota(jnp.int32, (4, V), 1) // TILE == lax.broadcasted_iota(jnp.int32, (4, V), 0)).astype(F32)
    for i in range(2):
        kept = lax.dot_general(
            mask_ref[i, vir // 8].astype(F32), spread, (((0,), (0,)), ((), ())), preferred_element_type=F32
        )
        amp_all[i, vir] = amp_ref[i] * kept[:, None, :]

    lane = lax.broadcasted_iota(jnp.int32, (NO, V), 1) // 16
    row = lax.broadcasted_iota(jnp.int32, (NO, V), 0)
    label = jnp.full((NO, V), irrep_ref[NO + occ // 4] ^ irrep_ref[NO + vir // 8], jnp.int32)
    lanes = jnp.zeros((NO, V), jnp.int32)
    rows = jnp.zeros((NO, V), jnp.int32)
    for k in range(KW):
        lanes = jnp.where(lane == k, irrep_ref[k], lanes)
    for j in range(NO):
        rows = jnp.where(row == j, irrep_ref[j], rows)
    symmetry = ((label ^ lanes ^ rows) == 0).astype(F32)
    for b in range(8):
        int_all[occ, b * NO : (b + 1) * NO, :] = int_ref[pl.ds(b, V, stride=8), :].T * symmetry

    pl.semaphore_wait(barrier, 20)

    count = [0]
    sent = []

    def move(source, to, landing):
        slot = count[0]
        count[0] += 1
        copy = pltpu.make_async_remote_copy(
            src_ref=source, dst_ref=source, send_sem=send_sem.at[slot], recv_sem=recv_sem.at[slot], device_id=to, device_id_type=MESH
        )
        copy.start()
        sent.append(copy)
        arrival = pltpu.make_async_remote_copy(
            src_ref=landing, dst_ref=landing, send_sem=send_sem.at[slot], recv_sem=recv_sem.at[slot], device_id=to, device_id_type=MESH
        )
        return arrival.wait_recv

    arrivals = []
    x_wait = {}
    y_wait = {}
    z_wait = {}

    def block(i, dx, dy, flip=0):
        return amp_all.at[i, vir_at(dx, dy, flip)]

    def half(i, dx, dy, upper):
        return amp_all.at[i, vir_at(dx, dy, 0), pl.ds(8 * upper, 8)]

    right, left = (occ, vir_at(1, 0, 0)), (occ, vir_at(-1, 0, 0))
    up, down = (occ, vir_at(0, 1, 0)), (occ, vir_at(0, -1, 0))
    sibling = (occ, vir_at(0, 0, 1))

    def share(i, dx, dy):
        arrivals.append(move(block(i, dx, dy), sibling, block(i, dx, dy, 1)))

    def x_start(i, dy):
        x_wait[i, dy] = (
            move(block(i, 0, dy), right, block(i, -1, dy)),
            move(block(i, 0, dy), left, block(i, 1, dy)),
        )
        share(i, 0, dy)

    def x_forward(i, dy):
        first, second = x_wait[i, dy]
        first()
        one = move(half(i, -1, dy, 0), right, half(i, 2, dy, 0))
        share(i, -1, dy)
        second()
        two = move(half(i, 1, dy, 1), left, half(i, 2, dy, 1))
        share(i, 1, dy)
        x_wait[i, dy] = (one, two)

    def x_end(i, dy):
        one, two = x_wait[i, dy]
        one()
        two()
        share(i, 2, dy)

    def y_start(i):
        y_wait[i] = [move(block(i, 0, 0), up, block(i, 0, -1)), move(block(i, 0, 0), down, block(i, 0, 1))]

    def y_forward(i):
        first, second = y_wait[i]
        first()
        one = move(half(i, 0, -1, 0), up, half(i, 0, 2, 0))
        x_start(i, -1)
        second()
        two = move(half(i, 0, 1, 1), down, half(i, 0, 2, 1))
        x_start(i, 1)
        y_wait[i] = [one, two]

    def y_end(i):
        one, two = y_wait[i]
        one()
        two()
        x_start(i, 2)

    above, below = (occ_at(1, 0), vir), (occ_at(-1, 0), vir)

    def z_start(flip):
        z_wait[flip] = (
            move(int_all.at[occ_at(0, flip)], above, int_all.at[occ_at(-1, flip)]),
            move(int_all.at[occ_at(0, flip)], below, int_all.at[occ_at(1, flip)]),
        )

    def z_forward(flip, hop):
        first, second = z_wait[flip]
        first()
        if hop < 3:
            one = move(int_all.at[occ_at(-hop, flip)], above, int_all.at[occ_at(-hop - 1, flip)])
        else:
            one = move(int_all.at[occ_at(-3, flip), pl.ds(0, 128)], above, int_all.at[occ_at(4, flip), pl.ds(0, 128)])
        second()
        if hop < 3:
            two = move(int_all.at[occ_at(hop, flip)], below, int_all.at[occ_at(hop + 1, flip)])
        else:
            two = move(int_all.at[occ_at(3, flip), pl.ds(128, 128)], below, int_all.at[occ_at(4, flip), pl.ds(128, 128)])
        z_wait[flip] = (one, two)

    def z_end(flip):
        one, two = z_wait[flip]
        one()
        two()

    pair_wait = move(int_all.at[occ], (occ_at(0, 1), vir), int_all.at[occ_at(0, 1)])
    z_start(0)
    y_start(0)
    x_start(0, 0)
    y_start(1)
    x_start(1, 0)
    x_forward(0, 0)
    pair_wait()
    z_start(1)
    z_forward(0, 1)
    y_forward(0)
    x_forward(1, 0)
    y_forward(1)
    z_forward(1, 1)
    x_forward(0, -1)
    x_forward(0, 1)
    y_end(0)
    z_forward(0, 2)
    x_end(0, 0)
    x_end(1, 0)
    y_end(1)
    x_forward(1, -1)
    z_forward(1, 2)
    x_forward(1, 1)
    x_forward(0, 2)
    z_forward(0, 3)
    x_forward(1, 2)
    x_end(0, -1)
    x_end(0, 1)
    x_end(1, -1)
    x_end(1, 1)
    z_forward(1, 3)
    x_end(0, 2)
    x_end(1, 2)
    z_end(0)
    z_end(1)
    for wait in arrivals:
        wait()

    acc[...] = jnp.zeros_like(acc)

    def contract(o, carry):
        int_high, int_low = split(int_all[o])
        left_side = jnp.concatenate([int_high, int_high, int_low], axis=1)
        for i in range(2):
            piece = jnp.concatenate([amp_all[i, 2 * o][:, None], amp_all[i, 2 * o + 1][:, None]], axis=1).reshape(V, V)
            amp_high, amp_low = split(piece)
            right_side = jnp.concatenate([amp_high, amp_low, amp_high], axis=0)
            acc[i] += jnp.dot(left_side, right_side, preferred_element_type=F32)
        return carry

    lax.fori_loop(0, 16, contract, 0)

    for i in range(2):
        for b in range(8):
            for h in range(2):
                cyc[i, h, pl.ds(b, NO, stride=8), :] = acc[i, b * NO : (b + 1) * NO, h * 128 : (h + 1) * 128]
    passed = []
    for i in range(2):
        for step in range(1, 16):
            slot = i * 15 + step - 1
            to, origin = (occ + step) % 16, (occ + 16 - step) % 16
            copy = pltpu.make_async_remote_copy(
                src_ref=cyc.at[i, :, pl.ds(16 * to, 16)],
                dst_ref=mirror.at[:, pl.ds((2 * occ + i) * 16, 16)],
                send_sem=pass_send.at[slot],
                recv_sem=pass_recv.at[slot],
                device_id=(to, vir),
                device_id_type=MESH,
            )
            copy.start()
            landing = mirror.at[:, pl.ds((2 * origin + i) * 16, 16)]
            passed.append(
                (
                    copy,
                    pltpu.make_async_remote_copy(
                        src_ref=landing,
                        dst_ref=landing,
                        send_sem=pass_send.at[slot],
                        recv_sem=pass_recv.at[slot],
                        device_id=(to, vir),
                        device_id_type=MESH,
                    ),
                )
            )
        mirror[:, pl.ds((2 * occ + i) * 16, 16), :] = cyc[i, :, pl.ds(16 * occ, 16), :]
    for copy, arrival in passed:
        arrival.wait_recv()
    for i in range(2):
        for b in range(8):
            for h in range(2):
                out_ref[i, b, :, h * 128 : (h + 1) * 128] = (
                    acc[i, b * NO : (b + 1) * NO, h * 128 : (h + 1) * 128] - mirror[h, pl.ds(i * 8 + b, NO, stride=16), :]
                )
    for copy in sent:
        copy.wait_send()
    for copy, arrival in passed:
        copy.wait_send()


def sparse_kernel(
    amp_hbm, int_hbm, mask_ref, irrep_ref, out_ref,
    amp_in, int_in, turned, slots, amp_all, int_all, high_all, low_all, wide, acc, cyc, mirror,
    in_sem, send_sem, recv_sem, pass_send, pass_recv,
):
    occ, vir = lax.axis_index("occ"), lax.axis_index("vir")
    z, yl = occ // 2, occ % 2
    x, yh, core = vir // 8, (vir // 2) % 4, vir % 2

    def occ_at(dz, flip):
        return ((z + dz + 8) % 8) * 2 + (yl + flip) % 2

    def vir_at(dx, dy, flip):
        return (((x + dx + 4) % 4) * 4 + (yh + dy + 4) % 4) * 2 + (core + flip) % 2

    barrier = pltpu.get_barrier_semaphore()
    for step in range(1, 16):
        pl.semaphore_signal(barrier, inc=1, device_id=((occ + step) % 16, vir), device_id_type=MESH)
    for dx, dy, flip in ((1, 0, 0), (-1, 0, 0), (0, 1, 0), (0, -1, 0), (0, 0, 1)):
        pl.semaphore_signal(barrier, inc=1, device_id=(occ, vir_at(dx, dy, flip)), device_id_type=MESH)
    load_int = pltpu.make_async_copy(int_hbm, int_in, in_sem.at[0])
    load_amp = pltpu.make_async_copy(amp_hbm, amp_in, in_sem.at[1])
    load_amp.start()
    load_int.start()

    lane = lax.broadcasted_iota(jnp.int32, (NO, V), 1) // 16
    row = lax.broadcasted_iota(jnp.int32, (NO, V), 0)
    labels = jnp.full((NO, V), irrep_ref[NO + vir // 8], jnp.int32)
    for k in range(KW):
        labels = jnp.where(lane == k, labels ^ irrep_ref[k], labels)
    for j in range(NO):
        labels = jnp.where(row == j, labels ^ irrep_ref[j], labels)
    below = (lax.broadcasted_iota(jnp.int32, (NO, NO), 1) < lax.broadcasted_iota(jnp.int32, (NO, NO), 0)).astype(F32)
    for tile in range(4):
        allowed = (labels ^ irrep_ref[NO + tile]) == 0
        rank = jnp.dot(below, allowed.astype(F32), preferred_element_type=F32)
        slots[tile] = jnp.where(allowed, rank.astype(jnp.int32), -1)

    spread = (lax.broadcasted_iota(jnp.int32, (4, V), 1) // TILE == lax.broadcasted_iota(jnp.int32, (4, V), 0)).astype(F32)
    load_amp.wait()
    for i in range(2):
        kept = lax.dot_general(
            mask_ref[i, vir // 8].astype(F32), spread, (((0,), (0,)), ((), ())), preferred_element_type=F32
        )
        amp_all[i, vir] = amp_in[i] * kept[:, None, :]

    load_int.wait()
    for b in range(8):
        turned[b] = int_in[pl.ds(b, V, stride=8), :].T
    depth = lax.broadcasted_iota(jnp.int32, (DEPTH, V), 0)

    def pack(b, carry):
        packed = jnp.zeros((DEPTH, V), F32)
        for j in range(NO):
            place = jnp.broadcast_to(slots[occ // 4, j : j + 1, :], (DEPTH, V))
            packed = jnp.where(place == depth, jnp.broadcast_to(turned[b, j : j + 1, :], (DEPTH, V)), packed)
        int_all[occ, b] = packed
        return carry

    lax.fori_loop(0, 8, pack, 0)
    pl.semaphore_wait(barrier, 20)

    count = [0]
    sent = []

    def move(source, to, landing):
        slot = count[0]
        count[0] += 1
        copy = pltpu.make_async_remote_copy(
            src_ref=source, dst_ref=source, send_sem=send_sem.at[slot], recv_sem=recv_sem.at[slot], device_id=to, device_id_type=MESH
        )
        copy.start()
        sent.append(copy)
        arrival = pltpu.make_async_remote_copy(
            src_ref=landing, dst_ref=landing, send_sem=send_sem.at[slot], recv_sem=recv_sem.at[slot], device_id=to, device_id_type=MESH
        )
        return arrival.wait_recv

    share_wait = {}
    x_wait = {}
    y_wait = {}
    z_wait = {}

    def block(i, dx, dy, flip=0):
        return amp_all.at[i, vir_at(dx, dy, flip)]

    def half(i, dx, dy, upper):
        return amp_all.at[i, vir_at(dx, dy, 0), pl.ds(8 * upper, 8)]

    right, left = (occ, vir_at(1, 0, 0)), (occ, vir_at(-1, 0, 0))
    up, down = (occ, vir_at(0, 1, 0)), (occ, vir_at(0, -1, 0))
    sibling = (occ, vir_at(0, 0, 1))

    def share(i, dx, dy):
        share_wait[i, dx, dy] = move(block(i, dx, dy), sibling, block(i, dx, dy, 1))

    def x_start(i, dy):
        x_wait[i, dy] = (
            move(block(i, 0, dy), right, block(i, -1, dy)),
            move(block(i, 0, dy), left, block(i, 1, dy)),
        )
        share(i, 0, dy)

    def x_forward(i, dy):
        first, second = x_wait[i, dy]
        first()
        one = move(half(i, -1, dy, 0), right, half(i, 2, dy, 0))
        share(i, -1, dy)
        second()
        two = move(half(i, 1, dy, 1), left, half(i, 2, dy, 1))
        share(i, 1, dy)
        x_wait[i, dy] = (one, two)

    def x_end(i, dy):
        one, two = x_wait[i, dy]
        one()
        two()
        share(i, 2, dy)

    def y_start(i):
        y_wait[i] = [move(block(i, 0, 0), up, block(i, 0, -1)), move(block(i, 0, 0), down, block(i, 0, 1))]

    def y_forward(i):
        first, second = y_wait[i]
        first()
        one = move(half(i, 0, -1, 0), up, half(i, 0, 2, 0))
        x_start(i, -1)
        second()
        two = move(half(i, 0, 1, 1), down, half(i, 0, 2, 1))
        x_start(i, 1)
        y_wait[i] = [one, two]

    def y_end(i):
        one, two = y_wait[i]
        one()
        two()
        x_start(i, 2)

    above, below_z = (occ_at(1, 0), vir), (occ_at(-1, 0), vir)

    def z_start(flip):
        z_wait[flip] = (
            move(int_all.at[occ_at(0, flip)], above, int_all.at[occ_at(-1, flip)]),
            move(int_all.at[occ_at(0, flip)], below_z, int_all.at[occ_at(1, flip)]),
        )

    def z_forward(flip, hop):
        first, second = z_wait[flip]
        first()
        if hop < 3:
            one = move(int_all.at[occ_at(-hop, flip)], above, int_all.at[occ_at(-hop - 1, flip)])
        else:
            one = move(int_all.at[occ_at(-3, flip), pl.ds(0, 4)], above, int_all.at[occ_at(4, flip), pl.ds(0, 4)])
        second()
        if hop < 3:
            two = move(int_all.at[occ_at(hop, flip)], below_z, int_all.at[occ_at(hop + 1, flip)])
        else:
            two = move(int_all.at[occ_at(3, flip), pl.ds(4, 4)], below_z, int_all.at[occ_at(4, flip), pl.ds(4, 4)])
        z_wait[flip] = (one, two)

    def z_end(flip):
        one, two = z_wait[flip]
        one()
        two()

    def unpack(*places):
        for dz, flip in places:
            o = occ_at(dz, flip)

            def one(b, carry, o=o):
                for g in range(4):
                    for h in range(2):
                        cols = pl.ds(128 * h, 128)
                        place = slots[o // 4, 8 * g : 8 * g + 8, cols]
                        near = jnp.take_along_axis(int_all[o, b, 0:8, cols], place & 7, axis=0)
                        far = jnp.take_along_axis(int_all[o, b, 8:16, cols], place & 7, axis=0)
                        value = jnp.where(place < 0, 0.0, jnp.where(place < 8, near, far))
                        wide[pl.ds(b * NO + 8 * g, 8), cols] = value
                return carry

            lax.fori_loop(0, 8, one, 0)
            high_all[o], low_all[o] = split(wide[...])

    def contract(i, dx, start=False):
        base = ((x + dx + 4) % 4) * 4

        def one(step, carry):
            o = base + step
            high = high_all[o]
            left_side = jnp.concatenate([high, high, low_all[o]], axis=1)
            piece = jnp.concatenate([amp_all[i, 2 * o][:, None], amp_all[i, 2 * o + 1][:, None]], axis=1).reshape(V, V)
            amp_high, amp_low = split(piece)
            right_side = jnp.concatenate([amp_high, amp_low, amp_high], axis=0)
            acc[i] += jnp.dot(left_side, right_side, preferred_element_type=F32)
            return carry

        for dy in (0, -1, 1, 2):
            share_wait[i, dx, dy]()
        if start:
            acc[i] = jnp.zeros((V, V), F32)
        lax.fori_loop(0, 4, one, 0)

    passed = []

    def exchange(i):
        for b in range(8):
            for h in range(2):
                cyc[i, h, pl.ds(b, NO, stride=8), :] = acc[i, b * NO : (b + 1) * NO, h * 128 : (h + 1) * 128]
        for step in FAR_FIRST:
            slot = i * 15 + step - 1
            to, origin = (occ + step) % 16, (occ + 16 - step) % 16
            copy = pltpu.make_async_remote_copy(
                src_ref=cyc.at[i, :, pl.ds(16 * to, 16)],
                dst_ref=mirror.at[:, pl.ds((2 * occ + i) * 16, 16)],
                send_sem=pass_send.at[slot],
                recv_sem=pass_recv.at[slot],
                device_id=(to, vir),
                device_id_type=MESH,
            )
            copy.start()
            landing = mirror.at[:, pl.ds((2 * origin + i) * 16, 16)]
            arrival = pltpu.make_async_remote_copy(
                src_ref=landing,
                dst_ref=landing,
                send_sem=pass_send.at[slot],
                recv_sem=pass_recv.at[slot],
                device_id=(to, vir),
                device_id_type=MESH,
            )
            passed.append((copy, arrival))
        mirror[:, pl.ds((2 * occ + i) * 16, 16), :] = cyc[i, :, pl.ds(16 * occ, 16), :]

    y_start(0)
    x_start(0, 0)
    z_start(0)
    pair_wait = move(int_all.at[occ], (occ_at(0, 1), vir), int_all.at[occ_at(0, 1)])
    x_start(1, 0)
    unpack((0, 0))
    x_forward(0, 0)
    z_forward(0, 1)
    y_forward(0)
    y_start(1)
    z_forward(0, 2)
    x_end(0, 0)
    pair_wait()
    z_start(1)
    z_forward(0, 3)
    x_forward(0, -1)
    y_end(0)
    unpack((1, 0), (-1, 0))
    z_forward(1, 1)
    x_forward(0, 1)
    z_end(0)
    unpack((2, 0), (-2, 0))
    x_forward(1, 0)
    z_forward(1, 2)
    x_forward(0, 2)
    y_forward(1)
    unpack((3, 0), (-3, 0))
    z_forward(1, 3)
    y_end(1)
    x_end(0, -1)
    x_end(0, 1)
    unpack((4, 0), (0, 1), (1, 1), (-1, 1))
    x_end(0, 2)
    x_end(1, 0)
    z_end(1)
    unpack((2, 1), (-2, 1), (3, 1), (-3, 1), (4, 1))
    contract(0, 0, True)
    contract(0, 1)
    contract(0, -1)
    contract(0, 2)
    exchange(0)
    x_forward(1, -1)
    contract(1, 0, True)
    x_forward(1, 1)
    x_forward(1, 2)
    contract(1, 1)
    contract(1, -1)
    x_end(1, -1)
    x_end(1, 1)
    x_end(1, 2)
    contract(1, 2)
    exchange(1)
    for copy in sent:
        copy.wait_send()
    for copy, arrival in passed:
        arrival.wait_recv()
    for i in range(2):
        for b in range(8):
            for h in range(2):
                out_ref[i, b, :, h * 128 : (h + 1) * 128] = (
                    acc[i, b * NO : (b + 1) * NO, h * 128 : (h + 1) * 128] - mirror[h, pl.ds(i * 8 + b, NO, stride=16), :]
                )
    for copy, arrival in passed:
        copy.wait_send()


MOVES = 2 * (4 + 16 + 16) + 17


def dense(amplitudes, flat_int, mask, tile_irrep):
    vmem = pl.BlockSpec(memory_space=pltpu.VMEM)
    return pl.pallas_call(
        dense_kernel,
        out_shape=jax.ShapeDtypeStruct((2, 8, NO, V), F32),
        in_specs=[vmem, vmem, vmem, pl.BlockSpec(memory_space=pltpu.SMEM)],
        out_specs=vmem,
        scratch_shapes=[
            pltpu.VMEM((2, 32, KW, 8, V), F32),
            pltpu.VMEM((16, V, V), F32),
            pltpu.VMEM((2, V, V), F32),
            pltpu.VMEM((2, 2, V, 128), F32),
            pltpu.VMEM((2, 2 * V, 128), F32),
            pltpu.SemaphoreType.DMA((MOVES,)),
            pltpu.SemaphoreType.DMA((MOVES,)),
            pltpu.SemaphoreType.DMA((30,)),
            pltpu.SemaphoreType.DMA((30,)),
        ],
        compiler_params=pltpu.CompilerParams(collective_id=0, has_side_effects=True, vmem_limit_bytes=48 << 20),
    )(amplitudes, flat_int, mask, tile_irrep)


def sparse(amplitudes, flat_int, mask, tile_irrep):
    vmem = pl.BlockSpec(memory_space=pltpu.VMEM)
    hbm = pl.BlockSpec(memory_space=pl.ANY)
    return pl.pallas_call(
        sparse_kernel,
        out_shape=jax.ShapeDtypeStruct((2, 8, NO, V), F32),
        in_specs=[hbm, hbm, vmem, pl.BlockSpec(memory_space=pltpu.SMEM)],
        out_specs=vmem,
        scratch_shapes=[
            pltpu.VMEM((2, KW, 8, V), F32),
            pltpu.VMEM((KW * 16 * 8, NO), F32),
            pltpu.VMEM((8, NO, V), F32),
            pltpu.VMEM((4, NO, V), jnp.int32),
            pltpu.VMEM((2, 32, KW, 8, V), F32),
            pltpu.VMEM((16, 8, DEPTH, V), F32),
            pltpu.VMEM((16, V, V), BF16),
            pltpu.VMEM((16, V, V), BF16),
            pltpu.VMEM((V, V), F32),
            pltpu.VMEM((2, V, V), F32),
            pltpu.VMEM((2, 2, V, 128), F32),
            pltpu.VMEM((2, 2 * V, 128), F32),
            pltpu.SemaphoreType.DMA((2,)),
            pltpu.SemaphoreType.DMA((MOVES,)),
            pltpu.SemaphoreType.DMA((MOVES,)),
            pltpu.SemaphoreType.DMA((30,)),
            pltpu.SemaphoreType.DMA((30,)),
        ],
        compiler_params=pltpu.CompilerParams(collective_id=1, has_side_effects=True, vmem_limit_bytes=56 << 20),
    )(amplitudes, flat_int, mask, tile_irrep)


def body(amplitudes, integrals, tile_mask, tile_irrep):
    flat_int = integrals.transpose(0, 1, 3, 2).reshape(KW * 16 * 8, NO)
    mask = tile_mask.transpose(0, 2, 3, 1)
    occupied = tile_irrep[:NO]
    largest = jnp.max(jnp.sum((occupied[:, None] == occupied[None, :]).astype(jnp.int32), axis=1))
    return lax.cond(largest <= DEPTH, sparse, dense, amplitudes, flat_int, mask, tile_irrep)


def solution(mesh):
    return jax.shard_map(
        body,
        mesh=mesh,
        in_specs=(
            P("occ", None, "vir", None),
            P(None, "occ", None, "vir"),
            P("occ", None, None, None),
            P(),
        ),
        out_specs=P("occ", "vir", None, None),
        check_vma=False,
    )
```

```python
import jax
import jax.numpy as jnp
from jax import lax
from jax.experimental import pallas as pl
from jax.experimental.pallas import tpu as pltpu
from jax.sharding import PartitionSpec as P

NO = 32
V = 256
TILE = 64
KW = 16
DEPTH = 16
FAR_FIRST = (8, 7, 9, 6, 10, 5, 11, 4, 12, 3, 13, 2, 14, 1, 15)
MESH = pl.DeviceIdType.MESH
F32 = jnp.float32
BF16 = jnp.bfloat16


def split(value):
    high = value.astype(BF16)
    return high, (value - high.astype(F32)).astype(BF16)


def dense_kernel(amp_ref, int_ref, mask_ref, irrep_ref, out_ref, amp_all, int_all, acc, cyc, mirror, send_sem, recv_sem, pass_send, pass_recv):
    occ, vir = lax.axis_index("occ"), lax.axis_index("vir")
    z, yl = occ // 2, occ % 2
    x, yh, core = vir // 8, (vir // 2) % 4, vir % 2

    def occ_at(dz, flip):
        return ((z + dz + 8) % 8) * 2 + (yl + flip) % 2

    def vir_at(dx, dy, flip):
        return (((x + dx + 4) % 4) * 4 + (yh + dy + 4) % 4) * 2 + (core + flip) % 2

    barrier = pltpu.get_barrier_semaphore()
    for step in range(1, 16):
        pl.semaphore_signal(barrier, inc=1, device_id=((occ + step) % 16, vir), device_id_type=MESH)
    for dx, dy, flip in ((1, 0, 0), (-1, 0, 0), (0, 1, 0), (0, -1, 0), (0, 0, 1)):
        pl.semaphore_signal(barrier, inc=1, device_id=(occ, vir_at(dx, dy, flip)), device_id_type=MESH)

    spread = (lax.broadcasted_iota(jnp.int32, (4, V), 1) // TILE == lax.broadcasted_iota(jnp.int32, (4, V), 0)).astype(F32)
    for i in range(2):
        kept = lax.dot_general(
            mask_ref[i, vir // 8].astype(F32), spread, (((0,), (0,)), ((), ())), preferred_element_type=F32
        )
        amp_all[i, vir] = amp_ref[i] * kept[:, None, :]

    lane = lax.broadcasted_iota(jnp.int32, (NO, V), 1) // 16
    row = lax.broadcasted_iota(jnp.int32, (NO, V), 0)
    label = jnp.full((NO, V), irrep_ref[NO + occ // 4] ^ irrep_ref[NO + vir // 8], jnp.int32)
    lanes = jnp.zeros((NO, V), jnp.int32)
    rows = jnp.zeros((NO, V), jnp.int32)
    for k in range(KW):
        lanes = jnp.where(lane == k, irrep_ref[k], lanes)
    for j in range(NO):
        rows = jnp.where(row == j, irrep_ref[j], rows)
    symmetry = ((label ^ lanes ^ rows) == 0).astype(F32)
    for b in range(8):
        int_all[occ, b * NO : (b + 1) * NO, :] = int_ref[pl.ds(b, V, stride=8), :].T * symmetry

    pl.semaphore_wait(barrier, 20)

    count = [0]
    sent = []

    def move(source, to, landing):
        slot = count[0]
        count[0] += 1
        copy = pltpu.make_async_remote_copy(
            src_ref=source, dst_ref=source, send_sem=send_sem.at[slot], recv_sem=recv_sem.at[slot], device_id=to, device_id_type=MESH
        )
        copy.start()
        sent.append(copy)
        arrival = pltpu.make_async_remote_copy(
            src_ref=landing, dst_ref=landing, send_sem=send_sem.at[slot], recv_sem=recv_sem.at[slot], device_id=to, device_id_type=MESH
        )
        return arrival.wait_recv

    arrivals = []
    x_wait = {}
    y_wait = {}
    z_wait = {}

    def block(i, dx, dy, flip=0):
        return amp_all.at[i, vir_at(dx, dy, flip)]

    def half(i, dx, dy, upper):
        return amp_all.at[i, vir_at(dx, dy, 0), pl.ds(8 * upper, 8)]

    right, left = (occ, vir_at(1, 0, 0)), (occ, vir_at(-1, 0, 0))
    up, down = (occ, vir_at(0, 1, 0)), (occ, vir_at(0, -1, 0))
    sibling = (occ, vir_at(0, 0, 1))

    def share(i, dx, dy):
        arrivals.append(move(block(i, dx, dy), sibling, block(i, dx, dy, 1)))

    def x_start(i, dy):
        x_wait[i, dy] = (
            move(block(i, 0, dy), right, block(i, -1, dy)),
            move(block(i, 0, dy), left, block(i, 1, dy)),
        )
        share(i, 0, dy)

    def x_forward(i, dy):
        first, second = x_wait[i, dy]
        first()
        one = move(half(i, -1, dy, 0), right, half(i, 2, dy, 0))
        share(i, -1, dy)
        second()
        two = move(half(i, 1, dy, 1), left, half(i, 2, dy, 1))
        share(i, 1, dy)
        x_wait[i, dy] = (one, two)

    def x_end(i, dy):
        one, two = x_wait[i, dy]
        one()
        two()
        share(i, 2, dy)

    def y_start(i):
        y_wait[i] = [move(block(i, 0, 0), up, block(i, 0, -1)), move(block(i, 0, 0), down, block(i, 0, 1))]

    def y_forward(i):
        first, second = y_wait[i]
        first()
        one = move(half(i, 0, -1, 0), up, half(i, 0, 2, 0))
        x_start(i, -1)
        second()
        two = move(half(i, 0, 1, 1), down, half(i, 0, 2, 1))
        x_start(i, 1)
        y_wait[i] = [one, two]

    def y_end(i):
        one, two = y_wait[i]
        one()
        two()
        x_start(i, 2)

    above, below = (occ_at(1, 0), vir), (occ_at(-1, 0), vir)

    def z_start(flip):
        z_wait[flip] = (
            move(int_all.at[occ_at(0, flip)], above, int_all.at[occ_at(-1, flip)]),
            move(int_all.at[occ_at(0, flip)], below, int_all.at[occ_at(1, flip)]),
        )

    def z_forward(flip, hop):
        first, second = z_wait[flip]
        first()
        if hop < 3:
            one = move(int_all.at[occ_at(-hop, flip)], above, int_all.at[occ_at(-hop - 1, flip)])
        else:
            one = move(int_all.at[occ_at(-3, flip), pl.ds(0, 128)], above, int_all.at[occ_at(4, flip), pl.ds(0, 128)])
        second()
        if hop < 3:
            two = move(int_all.at[occ_at(hop, flip)], below, int_all.at[occ_at(hop + 1, flip)])
        else:
            two = move(int_all.at[occ_at(3, flip), pl.ds(128, 128)], below, int_all.at[occ_at(4, flip), pl.ds(128, 128)])
        z_wait[flip] = (one, two)

    def z_end(flip):
        one, two = z_wait[flip]
        one()
        two()

    pair_wait = move(int_all.at[occ], (occ_at(0, 1), vir), int_all.at[occ_at(0, 1)])
    z_start(0)
    y_start(0)
    x_start(0, 0)
    y_start(1)
    x_start(1, 0)
    x_forward(0, 0)
    pair_wait()
    z_start(1)
    z_forward(0, 1)
    y_forward(0)
    x_forward(1, 0)
    y_forward(1)
    z_forward(1, 1)
    x_forward(0, -1)
    x_forward(0, 1)
    y_end(0)
    z_forward(0, 2)
    x_end(0, 0)
    x_end(1, 0)
    y_end(1)
    x_forward(1, -1)
    z_forward(1, 2)
    x_forward(1, 1)
    x_forward(0, 2)
    z_forward(0, 3)
    x_forward(1, 2)
    x_end(0, -1)
    x_end(0, 1)
    x_end(1, -1)
    x_end(1, 1)
    z_forward(1, 3)
    x_end(0, 2)
    x_end(1, 2)
    z_end(0)
    z_end(1)
    for wait in arrivals:
        wait()

    acc[...] = jnp.zeros_like(acc)

    def contract(o, carry):
        int_high, int_low = split(int_all[o])
        left_side = jnp.concatenate([int_high, int_high, int_low], axis=1)
        for i in range(2):
            piece = jnp.concatenate([amp_all[i, 2 * o][:, None], amp_all[i, 2 * o + 1][:, None]], axis=1).reshape(V, V)
            amp_high, amp_low = split(piece)
            right_side = jnp.concatenate([amp_high, amp_low, amp_high], axis=0)
            acc[i] += jnp.dot(left_side, right_side, preferred_element_type=F32)
        return carry

    lax.fori_loop(0, 16, contract, 0)

    for i in range(2):
        for b in range(8):
            for h in range(2):
                cyc[i, h, pl.ds(b, NO, stride=8), :] = acc[i, b * NO : (b + 1) * NO, h * 128 : (h + 1) * 128]
    passed = []
    for i in range(2):
        for step in range(1, 16):
            slot = i * 15 + step - 1
            to, origin = (occ + step) % 16, (occ + 16 - step) % 16
            copy = pltpu.make_async_remote_copy(
                src_ref=cyc.at[i, :, pl.ds(16 * to, 16)],
                dst_ref=mirror.at[:, pl.ds((2 * occ + i) * 16, 16)],
                send_sem=pass_send.at[slot],
                recv_sem=pass_recv.at[slot],
                device_id=(to, vir),
                device_id_type=MESH,
            )
            copy.start()
            landing = mirror.at[:, pl.ds((2 * origin + i) * 16, 16)]
            passed.append(
                (
                    copy,
                    pltpu.make_async_remote_copy(
                        src_ref=landing,
                        dst_ref=landing,
                        send_sem=pass_send.at[slot],
                        recv_sem=pass_recv.at[slot],
                        device_id=(to, vir),
                        device_id_type=MESH,
                    ),
                )
            )
        mirror[:, pl.ds((2 * occ + i) * 16, 16), :] = cyc[i, :, pl.ds(16 * occ, 16), :]
    for copy, arrival in passed:
        arrival.wait_recv()
    for i in range(2):
        for b in range(8):
            for h in range(2):
                out_ref[i, b, :, h * 128 : (h + 1) * 128] = (
                    acc[i, b * NO : (b + 1) * NO, h * 128 : (h + 1) * 128] - mirror[h, pl.ds(i * 8 + b, NO, stride=16), :]
                )
    for copy in sent:
        copy.wait_send()
    for copy, arrival in passed:
        copy.wait_send()


def sparse_kernel(
    amp_hbm, int_hbm, mask_ref, irrep_ref, out_ref,
    amp_in, int_in, turned, slots, amp_all, int_all, high_all, low_all, wide, acc, cyc, mirror,
    in_sem, send_sem, recv_sem, pass_send, pass_recv,
):
    occ, vir = lax.axis_index("occ"), lax.axis_index("vir")
    z, yl = occ // 2, occ % 2
    x, yh, core = vir // 8, (vir // 2) % 4, vir % 2

    def occ_at(dz, flip):
        return ((z + dz + 8) % 8) * 2 + (yl + flip) % 2

    def vir_at(dx, dy, flip):
        return (((x + dx + 4) % 4) * 4 + (yh + dy + 4) % 4) * 2 + (core + flip) % 2

    barrier = pltpu.get_barrier_semaphore()
    for step in range(1, 16):
        pl.semaphore_signal(barrier, inc=1, device_id=((occ + step) % 16, vir), device_id_type=MESH)
    for dx, dy, flip in ((1, 0, 0), (-1, 0, 0), (0, 1, 0), (0, -1, 0), (0, 0, 1)):
        pl.semaphore_signal(barrier, inc=1, device_id=(occ, vir_at(dx, dy, flip)), device_id_type=MESH)
    load_int = pltpu.make_async_copy(int_hbm, int_in, in_sem.at[0])
    load_amp = pltpu.make_async_copy(amp_hbm, amp_in, in_sem.at[1])
    load_amp.start()
    load_int.start()

    spread = (lax.broadcasted_iota(jnp.int32, (4, V), 1) // TILE == lax.broadcasted_iota(jnp.int32, (4, V), 0)).astype(F32)
    load_amp.wait()
    for i in range(2):
        kept = lax.dot_general(
            mask_ref[i, vir // 8].astype(F32), spread, (((0,), (0,)), ((), ())), preferred_element_type=F32
        )
        amp_all[i, vir] = amp_in[i] * kept[:, None, :]

    pl.semaphore_wait(barrier, 20)

    count = [0]
    sent = []

    def move(source, to, landing):
        slot = count[0]
        count[0] += 1
        copy = pltpu.make_async_remote_copy(
            src_ref=source, dst_ref=source, send_sem=send_sem.at[slot], recv_sem=recv_sem.at[slot], device_id=to, device_id_type=MESH
        )
        copy.start()
        sent.append(copy)
        arrival = pltpu.make_async_remote_copy(
            src_ref=landing, dst_ref=landing, send_sem=send_sem.at[slot], recv_sem=recv_sem.at[slot], device_id=to, device_id_type=MESH
        )
        return arrival.wait_recv

    share_wait = {}
    x_wait = {}
    y_wait = {}
    z_wait = {}

    def block(i, dx, dy, flip=0):
        return amp_all.at[i, vir_at(dx, dy, flip)]

    def half(i, dx, dy, upper):
        return amp_all.at[i, vir_at(dx, dy, 0), pl.ds(8 * upper, 8)]

    right, left = (occ, vir_at(1, 0, 0)), (occ, vir_at(-1, 0, 0))
    up, down = (occ, vir_at(0, 1, 0)), (occ, vir_at(0, -1, 0))
    sibling = (occ, vir_at(0, 0, 1))

    def share(i, dx, dy):
        share_wait[i, dx, dy] = move(block(i, dx, dy), sibling, block(i, dx, dy, 1))

    def x_start(i, dy):
        x_wait[i, dy] = (
            move(block(i, 0, dy), right, block(i, -1, dy)),
            move(block(i, 0, dy), left, block(i, 1, dy)),
        )
        share(i, 0, dy)

    def x_forward(i, dy):
        first, second = x_wait[i, dy]
        first()
        one = move(half(i, -1, dy, 0), right, half(i, 2, dy, 0))
        share(i, -1, dy)
        second()
        two = move(half(i, 1, dy, 1), left, half(i, 2, dy, 1))
        share(i, 1, dy)
        x_wait[i, dy] = (one, two)

    def x_end(i, dy):
        one, two = x_wait[i, dy]
        one()
        two()
        share(i, 2, dy)

    def y_start(i):
        y_wait[i] = [move(block(i, 0, 0), up, block(i, 0, -1)), move(block(i, 0, 0), down, block(i, 0, 1))]

    def y_forward(i):
        first, second = y_wait[i]
        first()
        one = move(half(i, 0, -1, 0), up, half(i, 0, 2, 0))
        x_start(i, -1)
        second()
        two = move(half(i, 0, 1, 1), down, half(i, 0, 2, 1))
        x_start(i, 1)
        y_wait[i] = [one, two]

    def y_end(i):
        one, two = y_wait[i]
        one()
        two()
        x_start(i, 2)

    above, below_z = (occ_at(1, 0), vir), (occ_at(-1, 0), vir)

    def piece(dz, flip, part):
        return int_all.at[occ_at(dz, flip), pl.ds(4 * part, 4)]

    def z_start(flip, part):
        z_wait[flip, part] = [
            move(piece(0, flip, part), above, piece(-1, flip, part)),
            move(piece(0, flip, part), below_z, piece(1, flip, part)),
        ]

    def z_forward(flip, hop, part):
        first, second = z_wait[flip, part]
        onward = []
        first()
        if hop < 3 or part == 0:
            onward.append(move(piece(-hop, flip, part), above, piece(-hop - 1, flip, part)))
        second()
        if hop < 3 or part == 1:
            onward.append(move(piece(hop, flip, part), below_z, piece(hop + 1, flip, part)))
        z_wait[flip, part] = onward

    def z_end(flip, part):
        for wait in z_wait[flip, part]:
            wait()

    def pair_start(part):
        z_wait["pair", part] = move(piece(0, 0, part), (occ_at(0, 1), vir), piece(0, 1, part))

    def pair_end(part):
        z_wait["pair", part]()
        z_start(1, part)

    def unpack(*places):
        for dz, flip in places:
            o = occ_at(dz, flip)

            def one(b, carry, o=o):
                for g in range(4):
                    for h in range(2):
                        cols = pl.ds(128 * h, 128)
                        place = slots[o // 4, 8 * g : 8 * g + 8, cols]
                        near = jnp.take_along_axis(int_all[o, b, 0:8, cols], place & 7, axis=0)
                        far = jnp.take_along_axis(int_all[o, b, 8:16, cols], place & 7, axis=0)
                        value = jnp.where(place < 0, 0.0, jnp.where(place < 8, near, far))
                        wide[pl.ds(b * NO + 8 * g, 8), cols] = value
                return carry

            lax.fori_loop(0, 8, one, 0)
            high_all[o], low_all[o] = split(wide[...])

    def contract(i, dx, start=False):
        base = ((x + dx + 4) % 4) * 4

        def one(step, carry):
            o = base + step
            high = high_all[o]
            left_side = jnp.concatenate([high, high, low_all[o]], axis=1)
            piece = jnp.concatenate([amp_all[i, 2 * o][:, None], amp_all[i, 2 * o + 1][:, None]], axis=1).reshape(V, V)
            amp_high, amp_low = split(piece)
            right_side = jnp.concatenate([amp_high, amp_low, amp_high], axis=0)
            acc[i] += jnp.dot(left_side, right_side, preferred_element_type=F32)
            return carry

        for dy in (0, -1, 1, 2):
            share_wait[i, dx, dy]()
        if start:
            acc[i] = jnp.zeros((V, V), F32)
        lax.fori_loop(0, 4, one, 0)

    passed = []

    def exchange(i):
        for b in range(8):
            for h in range(2):
                cyc[i, h, pl.ds(b, NO, stride=8), :] = acc[i, b * NO : (b + 1) * NO, h * 128 : (h + 1) * 128]
        for step in FAR_FIRST:
            slot = i * 15 + step - 1
            to, origin = (occ + step) % 16, (occ + 16 - step) % 16
            copy = pltpu.make_async_remote_copy(
                src_ref=cyc.at[i, :, pl.ds(16 * to, 16)],
                dst_ref=mirror.at[:, pl.ds((2 * occ + i) * 16, 16)],
                send_sem=pass_send.at[slot],
                recv_sem=pass_recv.at[slot],
                device_id=(to, vir),
                device_id_type=MESH,
            )
            copy.start()
            landing = mirror.at[:, pl.ds((2 * origin + i) * 16, 16)]
            arrival = pltpu.make_async_remote_copy(
                src_ref=landing,
                dst_ref=landing,
                send_sem=pass_send.at[slot],
                recv_sem=pass_recv.at[slot],
                device_id=(to, vir),
                device_id_type=MESH,
            )
            passed.append((copy, arrival))
        mirror[:, pl.ds((2 * occ + i) * 16, 16), :] = cyc[i, :, pl.ds(16 * occ, 16), :]

    y_start(0)
    x_start(0, 0)
    x_start(1, 0)

    lane = lax.broadcasted_iota(jnp.int32, (NO, V), 1) // 16
    row = lax.broadcasted_iota(jnp.int32, (NO, V), 0)
    labels = jnp.full((NO, V), irrep_ref[NO + vir // 8], jnp.int32)
    for k in range(KW):
        labels = jnp.where(lane == k, labels ^ irrep_ref[k], labels)
    for j in range(NO):
        labels = jnp.where(row == j, labels ^ irrep_ref[j], labels)
    below = (lax.broadcasted_iota(jnp.int32, (NO, NO), 1) < lax.broadcasted_iota(jnp.int32, (NO, NO), 0)).astype(F32)
    for tile in range(4):
        allowed = (labels ^ irrep_ref[NO + tile]) == 0
        rank = jnp.dot(below, allowed.astype(F32), preferred_element_type=F32)
        slots[tile] = jnp.where(allowed, rank.astype(jnp.int32), -1)

    load_int.wait()
    for b in range(8):
        turned[b] = int_in[pl.ds(b, V, stride=8), :].T
    depth = lax.broadcasted_iota(jnp.int32, (DEPTH, V), 0)

    def pack(b, carry):
        packed = jnp.zeros((DEPTH, V), F32)
        for j in range(NO):
            place = jnp.broadcast_to(slots[occ // 4, j : j + 1, :], (DEPTH, V))
            packed = jnp.where(place == depth, jnp.broadcast_to(turned[b, j : j + 1, :], (DEPTH, V)), packed)
        int_all[occ, b] = packed
        return carry

    lax.fori_loop(0, 8, pack, 0)
    z_start(0, 0)
    z_start(0, 1)
    pair_start(0)
    pair_start(1)
    unpack((0, 0))
    z_forward(0, 1, 0)
    x_forward(0, 0)
    z_forward(0, 1, 1)
    z_forward(0, 2, 0)
    y_forward(0)
    y_start(1)
    z_forward(0, 2, 1)
    x_end(0, 0)
    pair_end(0)
    z_forward(0, 3, 0)
    pair_end(1)
    z_forward(0, 3, 1)
    x_forward(0, -1)
    z_forward(1, 1, 0)
    y_end(0)
    z_forward(1, 1, 1)
    z_end(0, 0)
    z_end(0, 1)
    unpack((1, 0), (-1, 0), (2, 0), (-2, 0))
    x_forward(0, 1)
    z_forward(1, 2, 0)
    unpack((3, 0), (-3, 0), (4, 0), (0, 1))
    x_forward(1, 0)
    z_forward(1, 2, 1)
    y_forward(1)
    z_forward(1, 3, 0)
    x_forward(0, 2)
    z_forward(1, 3, 1)
    unpack((1, 1), (-1, 1), (2, 1), (-2, 1))
    x_end(0, -1)
    x_end(0, 1)
    unpack((3, 1), (-3, 1))
    z_end(1, 0)
    z_end(1, 1)
    unpack((4, 1))
    contract(0, 0, True)
    y_end(1)
    x_end(0, 2)
    contract(0, 1)
    contract(0, -1)
    x_forward(1, -1)
    contract(0, 2)
    exchange(0)
    x_end(1, 0)
    x_forward(1, 1)
    contract(1, 0, True)
    x_forward(1, 2)
    x_end(1, -1)
    contract(1, 1)
    x_end(1, 1)
    contract(1, -1)
    x_end(1, 2)
    contract(1, 2)
    exchange(1)
    for copy in sent:
        copy.wait_send()
    for copy, arrival in passed:
        arrival.wait_recv()
    for i in range(2):
        for b in range(8):
            for h in range(2):
                out_ref[i, b, :, h * 128 : (h + 1) * 128] = (
                    acc[i, b * NO : (b + 1) * NO, h * 128 : (h + 1) * 128] - mirror[h, pl.ds(i * 8 + b, NO, stride=16), :]
                )
    for copy, arrival in passed:
        copy.wait_send()


MOVES = 2 * (4 + 16 + 16) + 17


def dense(amplitudes, flat_int, mask, tile_irrep):
    vmem = pl.BlockSpec(memory_space=pltpu.VMEM)
    return pl.pallas_call(
        dense_kernel,
        out_shape=jax.ShapeDtypeStruct((2, 8, NO, V), F32),
        in_specs=[vmem, vmem, vmem, pl.BlockSpec(memory_space=pltpu.SMEM)],
        out_specs=vmem,
        scratch_shapes=[
            pltpu.VMEM((2, 32, KW, 8, V), F32),
            pltpu.VMEM((16, V, V), F32),
            pltpu.VMEM((2, V, V), F32),
            pltpu.VMEM((2, 2, V, 128), F32),
            pltpu.VMEM((2, 2 * V, 128), F32),
            pltpu.SemaphoreType.DMA((MOVES,)),
            pltpu.SemaphoreType.DMA((MOVES,)),
            pltpu.SemaphoreType.DMA((30,)),
            pltpu.SemaphoreType.DMA((30,)),
        ],
        compiler_params=pltpu.CompilerParams(collective_id=0, has_side_effects=True, vmem_limit_bytes=48 << 20),
    )(amplitudes, flat_int, mask, tile_irrep)


def sparse(amplitudes, flat_int, mask, tile_irrep):
    vmem = pl.BlockSpec(memory_space=pltpu.VMEM)
    hbm = pl.BlockSpec(memory_space=pl.ANY)
    return pl.pallas_call(
        sparse_kernel,
        out_shape=jax.ShapeDtypeStruct((2, 8, NO, V), F32),
        in_specs=[hbm, hbm, vmem, pl.BlockSpec(memory_space=pltpu.SMEM)],
        out_specs=vmem,
        scratch_shapes=[
            pltpu.VMEM((2, KW, 8, V), F32),
            pltpu.VMEM((KW * 16 * 8, NO), F32),
            pltpu.VMEM((8, NO, V), F32),
            pltpu.VMEM((4, NO, V), jnp.int32),
            pltpu.VMEM((2, 32, KW, 8, V), F32),
            pltpu.VMEM((16, 8, DEPTH, V), F32),
            pltpu.VMEM((16, V, V), BF16),
            pltpu.VMEM((16, V, V), BF16),
            pltpu.VMEM((V, V), F32),
            pltpu.VMEM((2, V, V), F32),
            pltpu.VMEM((2, 2, V, 128), F32),
            pltpu.VMEM((2, 2 * V, 128), F32),
            pltpu.SemaphoreType.DMA((2,)),
            pltpu.SemaphoreType.DMA((MOVES + 13,)),
            pltpu.SemaphoreType.DMA((MOVES + 13,)),
            pltpu.SemaphoreType.DMA((30,)),
            pltpu.SemaphoreType.DMA((30,)),
        ],
        compiler_params=pltpu.CompilerParams(collective_id=1, has_side_effects=True, vmem_limit_bytes=56 << 20),
    )(amplitudes, flat_int, mask, tile_irrep)


def body(amplitudes, integrals, tile_mask, tile_irrep):
    flat_int = integrals.transpose(0, 1, 3, 2).reshape(KW * 16 * 8, NO)
    mask = tile_mask.transpose(0, 2, 3, 1)
    occupied = tile_irrep[:NO]
    pairs = jnp.sum((occupied[:, None] == occupied[None, :]).astype(jnp.int32))
    return lax.cond(pairs < (DEPTH + 1) ** 2, sparse, dense, amplitudes, flat_int, mask, tile_irrep)


def solution(mesh):
    return jax.shard_map(
        body,
        mesh=mesh,
        in_specs=(
            P("occ", None, "vir", None),
            P(None, "occ", None, "vir"),
            P("occ", None, None, None),
            P(),
        ),
        out_specs=P("occ", "vir", None, None),
        check_vma=False,
    )
```

```python
import jax
import jax.numpy as jnp
from jax import lax
from jax.experimental import pallas as pl
from jax.experimental.pallas import tpu as pltpu
from jax.sharding import PartitionSpec as P

NO = 32
V = 256
TILE = 64
KW = 16
DEPTH = 16
FAR_FIRST = (8, 7, 9, 6, 10, 5, 11, 4, 12, 3, 13, 2, 14, 1, 15)
MESH = pl.DeviceIdType.MESH
F32 = jnp.float32
BF16 = jnp.bfloat16


def split(value):
    high = value.astype(BF16)
    return high, (value - high.astype(F32)).astype(BF16)


def dense_kernel(amp_ref, int_ref, mask_ref, irrep_ref, out_ref, amp_all, int_all, acc, cyc, mirror, send_sem, recv_sem, pass_send, pass_recv):
    occ, vir = lax.axis_index("occ"), lax.axis_index("vir")
    z, yl = occ // 2, occ % 2
    x, yh, core = vir // 8, (vir // 2) % 4, vir % 2

    def occ_at(dz, flip):
        return ((z + dz + 8) % 8) * 2 + (yl + flip) % 2

    def vir_at(dx, dy, flip):
        return (((x + dx + 4) % 4) * 4 + (yh + dy + 4) % 4) * 2 + (core + flip) % 2

    barrier = pltpu.get_barrier_semaphore()
    for step in range(1, 16):
        pl.semaphore_signal(barrier, inc=1, device_id=((occ + step) % 16, vir), device_id_type=MESH)
    for dx, dy, flip in ((1, 0, 0), (-1, 0, 0), (0, 1, 0), (0, -1, 0), (0, 0, 1)):
        pl.semaphore_signal(barrier, inc=1, device_id=(occ, vir_at(dx, dy, flip)), device_id_type=MESH)

    spread = (lax.broadcasted_iota(jnp.int32, (4, V), 1) // TILE == lax.broadcasted_iota(jnp.int32, (4, V), 0)).astype(F32)
    for i in range(2):
        kept = lax.dot_general(
            mask_ref[i, vir // 8].astype(F32), spread, (((0,), (0,)), ((), ())), preferred_element_type=F32
        )
        amp_all[i, vir] = amp_ref[i] * kept[:, None, :]

    lane = lax.broadcasted_iota(jnp.int32, (NO, V), 1) // 16
    row = lax.broadcasted_iota(jnp.int32, (NO, V), 0)
    label = jnp.full((NO, V), irrep_ref[NO + occ // 4] ^ irrep_ref[NO + vir // 8], jnp.int32)
    lanes = jnp.zeros((NO, V), jnp.int32)
    rows = jnp.zeros((NO, V), jnp.int32)
    for k in range(KW):
        lanes = jnp.where(lane == k, irrep_ref[k], lanes)
    for j in range(NO):
        rows = jnp.where(row == j, irrep_ref[j], rows)
    symmetry = ((label ^ lanes ^ rows) == 0).astype(F32)
    for b in range(8):
        int_all[occ, b * NO : (b + 1) * NO, :] = int_ref[pl.ds(b, V, stride=8), :].T * symmetry

    pl.semaphore_wait(barrier, 20)

    count = [0]
    sent = []

    def move(source, to, landing):
        slot = count[0]
        count[0] += 1
        copy = pltpu.make_async_remote_copy(
            src_ref=source, dst_ref=source, send_sem=send_sem.at[slot], recv_sem=recv_sem.at[slot], device_id=to, device_id_type=MESH
        )
        copy.start()
        sent.append(copy)
        arrival = pltpu.make_async_remote_copy(
            src_ref=landing, dst_ref=landing, send_sem=send_sem.at[slot], recv_sem=recv_sem.at[slot], device_id=to, device_id_type=MESH
        )
        return arrival.wait_recv

    arrivals = []
    x_wait = {}
    y_wait = {}
    z_wait = {}

    def block(i, dx, dy, flip=0):
        return amp_all.at[i, vir_at(dx, dy, flip)]

    def half(i, dx, dy, upper):
        return amp_all.at[i, vir_at(dx, dy, 0), pl.ds(8 * upper, 8)]

    right, left = (occ, vir_at(1, 0, 0)), (occ, vir_at(-1, 0, 0))
    up, down = (occ, vir_at(0, 1, 0)), (occ, vir_at(0, -1, 0))
    sibling = (occ, vir_at(0, 0, 1))

    def share(i, dx, dy):
        arrivals.append(move(block(i, dx, dy), sibling, block(i, dx, dy, 1)))

    def x_start(i, dy):
        x_wait[i, dy] = (
            move(block(i, 0, dy), right, block(i, -1, dy)),
            move(block(i, 0, dy), left, block(i, 1, dy)),
        )
        share(i, 0, dy)

    def x_forward(i, dy):
        first, second = x_wait[i, dy]
        first()
        one = move(half(i, -1, dy, 0), right, half(i, 2, dy, 0))
        share(i, -1, dy)
        second()
        two = move(half(i, 1, dy, 1), left, half(i, 2, dy, 1))
        share(i, 1, dy)
        x_wait[i, dy] = (one, two)

    def x_end(i, dy):
        one, two = x_wait[i, dy]
        one()
        two()
        share(i, 2, dy)

    def y_start(i):
        y_wait[i] = [move(block(i, 0, 0), up, block(i, 0, -1)), move(block(i, 0, 0), down, block(i, 0, 1))]

    def y_forward(i):
        first, second = y_wait[i]
        first()
        one = move(half(i, 0, -1, 0), up, half(i, 0, 2, 0))
        x_start(i, -1)
        second()
        two = move(half(i, 0, 1, 1), down, half(i, 0, 2, 1))
        x_start(i, 1)
        y_wait[i] = [one, two]

    def y_end(i):
        one, two = y_wait[i]
        one()
        two()
        x_start(i, 2)

    above, below = (occ_at(1, 0), vir), (occ_at(-1, 0), vir)

    def z_start(flip):
        z_wait[flip] = (
            move(int_all.at[occ_at(0, flip)], above, int_all.at[occ_at(-1, flip)]),
            move(int_all.at[occ_at(0, flip)], below, int_all.at[occ_at(1, flip)]),
        )

    def z_forward(flip, hop):
        first, second = z_wait[flip]
        first()
        if hop < 3:
            one = move(int_all.at[occ_at(-hop, flip)], above, int_all.at[occ_at(-hop - 1, flip)])
        else:
            one = move(int_all.at[occ_at(-3, flip), pl.ds(0, 128)], above, int_all.at[occ_at(4, flip), pl.ds(0, 128)])
        second()
        if hop < 3:
            two = move(int_all.at[occ_at(hop, flip)], below, int_all.at[occ_at(hop + 1, flip)])
        else:
            two = move(int_all.at[occ_at(3, flip), pl.ds(128, 128)], below, int_all.at[occ_at(4, flip), pl.ds(128, 128)])
        z_wait[flip] = (one, two)

    def z_end(flip):
        one, two = z_wait[flip]
        one()
        two()

    pair_wait = move(int_all.at[occ], (occ_at(0, 1), vir), int_all.at[occ_at(0, 1)])
    z_start(0)
    y_start(0)
    x_start(0, 0)
    y_start(1)
    x_start(1, 0)
    x_forward(0, 0)
    pair_wait()
    z_start(1)
    z_forward(0, 1)
    y_forward(0)
    x_forward(1, 0)
    y_forward(1)
    z_forward(1, 1)
    x_forward(0, -1)
    x_forward(0, 1)
    y_end(0)
    z_forward(0, 2)
    x_end(0, 0)
    x_end(1, 0)
    y_end(1)
    x_forward(1, -1)
    z_forward(1, 2)
    x_forward(1, 1)
    x_forward(0, 2)
    z_forward(0, 3)
    x_forward(1, 2)
    x_end(0, -1)
    x_end(0, 1)
    x_end(1, -1)
    x_end(1, 1)
    z_forward(1, 3)
    x_end(0, 2)
    x_end(1, 2)
    z_end(0)
    z_end(1)
    for wait in arrivals:
        wait()

    acc[...] = jnp.zeros_like(acc)

    def contract(o, carry):
        int_high, int_low = split(int_all[o])
        left_side = jnp.concatenate([int_high, int_high, int_low], axis=1)
        for i in range(2):
            piece = jnp.concatenate([amp_all[i, 2 * o][:, None], amp_all[i, 2 * o + 1][:, None]], axis=1).reshape(V, V)
            amp_high, amp_low = split(piece)
            right_side = jnp.concatenate([amp_high, amp_low, amp_high], axis=0)
            acc[i] += jnp.dot(left_side, right_side, preferred_element_type=F32)
        return carry

    lax.fori_loop(0, 16, contract, 0)

    for i in range(2):
        for b in range(8):
            for h in range(2):
                cyc[i, h, pl.ds(b, NO, stride=8), :] = acc[i, b * NO : (b + 1) * NO, h * 128 : (h + 1) * 128]
    passed = []
    for i in range(2):
        for step in range(1, 16):
            slot = i * 15 + step - 1
            to, origin = (occ + step) % 16, (occ + 16 - step) % 16
            copy = pltpu.make_async_remote_copy(
                src_ref=cyc.at[i, :, pl.ds(16 * to, 16)],
                dst_ref=mirror.at[:, pl.ds((2 * occ + i) * 16, 16)],
                send_sem=pass_send.at[slot],
                recv_sem=pass_recv.at[slot],
                device_id=(to, vir),
                device_id_type=MESH,
            )
            copy.start()
            landing = mirror.at[:, pl.ds((2 * origin + i) * 16, 16)]
            passed.append(
                (
                    copy,
                    pltpu.make_async_remote_copy(
                        src_ref=landing,
                        dst_ref=landing,
                        send_sem=pass_send.at[slot],
                        recv_sem=pass_recv.at[slot],
                        device_id=(to, vir),
                        device_id_type=MESH,
                    ),
                )
            )
        mirror[:, pl.ds((2 * occ + i) * 16, 16), :] = cyc[i, :, pl.ds(16 * occ, 16), :]
    for copy, arrival in passed:
        arrival.wait_recv()
    for i in range(2):
        for b in range(8):
            for h in range(2):
                out_ref[i, b, :, h * 128 : (h + 1) * 128] = (
                    acc[i, b * NO : (b + 1) * NO, h * 128 : (h + 1) * 128] - mirror[h, pl.ds(i * 8 + b, NO, stride=16), :]
                )
    for copy in sent:
        copy.wait_send()
    for copy, arrival in passed:
        copy.wait_send()


def sparse_kernel(
    amp_hbm, int_hbm, mask_ref, irrep_ref, out_ref,
    amp_in, int_in, turned, slots, amp_all, int_all, high_all, low_all, wide, acc, cyc, mirror,
    in_sem, send_sem, recv_sem, pass_send, pass_recv,
):
    occ, vir = lax.axis_index("occ"), lax.axis_index("vir")
    z, yl = occ // 2, occ % 2
    x, yh, core = vir // 8, (vir // 2) % 4, vir % 2

    def occ_at(dz, flip):
        return ((z + dz + 8) % 8) * 2 + (yl + flip) % 2

    def vir_at(dx, dy, flip):
        return (((x + dx + 4) % 4) * 4 + (yh + dy + 4) % 4) * 2 + (core + flip) % 2

    barrier = pltpu.get_barrier_semaphore()
    for step in range(1, 16):
        pl.semaphore_signal(barrier, inc=1, device_id=((occ + step) % 16, vir), device_id_type=MESH)
    for dx, dy, flip in ((1, 0, 0), (-1, 0, 0), (0, 1, 0), (0, -1, 0), (0, 0, 1)):
        pl.semaphore_signal(barrier, inc=1, device_id=(occ, vir_at(dx, dy, flip)), device_id_type=MESH)
    load_int = pltpu.make_async_copy(int_hbm, int_in, in_sem.at[0])
    load_amp = pltpu.make_async_copy(amp_hbm, amp_in, in_sem.at[1])
    load_amp.start()
    load_int.start()

    spread = (lax.broadcasted_iota(jnp.int32, (4, V), 1) // TILE == lax.broadcasted_iota(jnp.int32, (4, V), 0)).astype(F32)
    load_amp.wait()
    for i in range(2):
        kept = lax.dot_general(
            mask_ref[i, vir // 8].astype(F32), spread, (((0,), (0,)), ((), ())), preferred_element_type=F32
        )
        amp_all[i, vir] = amp_in[i] * kept[:, None, :]

    pl.semaphore_wait(barrier, 20)

    count = [0]
    sent = []

    def move(source, to, landing):
        slot = count[0]
        count[0] += 1
        copy = pltpu.make_async_remote_copy(
            src_ref=source, dst_ref=source, send_sem=send_sem.at[slot], recv_sem=recv_sem.at[slot], device_id=to, device_id_type=MESH
        )
        copy.start()
        sent.append(copy)
        arrival = pltpu.make_async_remote_copy(
            src_ref=landing, dst_ref=landing, send_sem=send_sem.at[slot], recv_sem=recv_sem.at[slot], device_id=to, device_id_type=MESH
        )
        return arrival.wait_recv

    share_wait = {}
    x_wait = {}
    y_wait = {}
    z_wait = {}

    def block(i, dx, dy, flip=0):
        return amp_all.at[i, vir_at(dx, dy, flip)]

    def half(i, dx, dy, upper):
        return amp_all.at[i, vir_at(dx, dy, 0), pl.ds(8 * upper, 8)]

    right, left = (occ, vir_at(1, 0, 0)), (occ, vir_at(-1, 0, 0))
    up, down = (occ, vir_at(0, 1, 0)), (occ, vir_at(0, -1, 0))
    sibling = (occ, vir_at(0, 0, 1))

    def share(i, dx, dy):
        share_wait[i, dx, dy] = move(block(i, dx, dy), sibling, block(i, dx, dy, 1))

    def x_start(i, dy):
        x_wait[i, dy] = (
            move(block(i, 0, dy), right, block(i, -1, dy)),
            move(block(i, 0, dy), left, block(i, 1, dy)),
        )
        share(i, 0, dy)

    def x_forward(i, dy):
        first, second = x_wait[i, dy]
        first()
        one = move(half(i, -1, dy, 0), right, half(i, 2, dy, 0))
        share(i, -1, dy)
        second()
        two = move(half(i, 1, dy, 1), left, half(i, 2, dy, 1))
        share(i, 1, dy)
        x_wait[i, dy] = (one, two)

    def x_end(i, dy):
        one, two = x_wait[i, dy]
        one()
        two()
        share(i, 2, dy)

    def y_start(i):
        y_wait[i] = [move(block(i, 0, 0), up, block(i, 0, -1)), move(block(i, 0, 0), down, block(i, 0, 1))]

    def y_forward(i):
        first, second = y_wait[i]
        first()
        one = move(half(i, 0, -1, 0), up, half(i, 0, 2, 0))
        x_start(i, -1)
        second()
        two = move(half(i, 0, 1, 1), down, half(i, 0, 2, 1))
        x_start(i, 1)
        y_wait[i] = [one, two]

    def y_end(i):
        one, two = y_wait[i]
        one()
        two()
        x_start(i, 2)

    above, below_z = (occ_at(1, 0), vir), (occ_at(-1, 0), vir)

    def piece(dz, flip, part):
        return int_all.at[occ_at(dz, flip), pl.ds(4 * part, 4)]

    def z_start(flip, part):
        z_wait[flip, part] = [
            move(piece(0, flip, part), above, piece(-1, flip, part)),
            move(piece(0, flip, part), below_z, piece(1, flip, part)),
        ]

    def z_forward(flip, hop, part):
        first, second = z_wait[flip, part]
        onward = []
        first()
        if hop < 3 or part == 0:
            onward.append(move(piece(-hop, flip, part), above, piece(-hop - 1, flip, part)))
        second()
        if hop < 3 or part == 1:
            onward.append(move(piece(hop, flip, part), below_z, piece(hop + 1, flip, part)))
        z_wait[flip, part] = onward

    def z_end(flip, part):
        for wait in z_wait[flip, part]:
            wait()

    def pair_start(part):
        z_wait["pair", part] = move(piece(0, 0, part), (occ_at(0, 1), vir), piece(0, 1, part))

    def pair_end(part):
        z_wait["pair", part]()
        z_start(1, part)

    def unpack(*places):
        for dz, flip in places:
            o = occ_at(dz, flip)

            def one(b, carry, o=o):
                for g in range(4):
                    for h in range(2):
                        cols = pl.ds(128 * h, 128)
                        place = slots[o // 4, 8 * g : 8 * g + 8, cols]
                        near = jnp.take_along_axis(int_all[o, b, 0:8, cols], place & 7, axis=0)
                        far = jnp.take_along_axis(int_all[o, b, 8:16, cols], place & 7, axis=0)
                        value = jnp.where(place < 0, 0.0, jnp.where(place < 8, near, far))
                        wide[pl.ds(b * NO + 8 * g, 8), cols] = value
                return carry

            lax.fori_loop(0, 8, one, 0)
            high_all[o], low_all[o] = split(wide[...])

    def contract(i, dx, start=False, first=-1, count=4):
        base = ((x + dx + 4) % 4) * 4

        def one(step, carry):
            o = base + (yh + first + step + 4) % 4
            high = high_all[o]
            left_side = jnp.concatenate([high, high, low_all[o]], axis=1)
            piece = jnp.concatenate([amp_all[i, 2 * o][:, None], amp_all[i, 2 * o + 1][:, None]], axis=1).reshape(V, V)
            amp_high, amp_low = split(piece)
            right_side = jnp.concatenate([amp_high, amp_low, amp_high], axis=0)
            acc[i] += jnp.dot(left_side, right_side, preferred_element_type=F32)
            return carry

        for dy in range(first, first + count):
            share_wait[i, dx, dy]()
        if start:
            acc[i] = jnp.zeros((V, V), F32)
        lax.fori_loop(0, count, one, 0)

    passed = []

    def exchange(i):
        for b in range(8):
            for h in range(2):
                cyc[i, h, pl.ds(b, NO, stride=8), :] = acc[i, b * NO : (b + 1) * NO, h * 128 : (h + 1) * 128]
        for step in FAR_FIRST:
            slot = i * 15 + step - 1
            to, origin = (occ + step) % 16, (occ + 16 - step) % 16
            copy = pltpu.make_async_remote_copy(
                src_ref=cyc.at[i, :, pl.ds(16 * to, 16)],
                dst_ref=mirror.at[:, pl.ds((2 * occ + i) * 16, 16)],
                send_sem=pass_send.at[slot],
                recv_sem=pass_recv.at[slot],
                device_id=(to, vir),
                device_id_type=MESH,
            )
            copy.start()
            landing = mirror.at[:, pl.ds((2 * origin + i) * 16, 16)]
            arrival = pltpu.make_async_remote_copy(
                src_ref=landing,
                dst_ref=landing,
                send_sem=pass_send.at[slot],
                recv_sem=pass_recv.at[slot],
                device_id=(to, vir),
                device_id_type=MESH,
            )
            passed.append((copy, arrival))
        mirror[:, pl.ds((2 * occ + i) * 16, 16), :] = cyc[i, :, pl.ds(16 * occ, 16), :]

    y_start(0)
    x_start(0, 0)
    x_start(1, 0)

    lane = lax.broadcasted_iota(jnp.int32, (NO, V), 1) // 16
    row = lax.broadcasted_iota(jnp.int32, (NO, V), 0)
    labels = jnp.full((NO, V), irrep_ref[NO + vir // 8], jnp.int32)
    for k in range(KW):
        labels = jnp.where(lane == k, labels ^ irrep_ref[k], labels)
    for j in range(NO):
        labels = jnp.where(row == j, labels ^ irrep_ref[j], labels)
    below = (lax.broadcasted_iota(jnp.int32, (NO, NO), 1) < lax.broadcasted_iota(jnp.int32, (NO, NO), 0)).astype(F32)
    for tile in range(4):
        allowed = (labels ^ irrep_ref[NO + tile]) == 0
        rank = jnp.dot(below, allowed.astype(F32), preferred_element_type=F32)
        slots[tile] = jnp.where(allowed, rank.astype(jnp.int32), -1)

    load_int.wait()
    for b in range(8):
        turned[b] = int_in[pl.ds(b, V, stride=8), :].T
    depth = lax.broadcasted_iota(jnp.int32, (DEPTH, V), 0)

    def pack(b, carry):
        packed = jnp.zeros((DEPTH, V), F32)
        for j in range(NO):
            place = jnp.broadcast_to(slots[occ // 4, j : j + 1, :], (DEPTH, V))
            packed = jnp.where(place == depth, jnp.broadcast_to(turned[b, j : j + 1, :], (DEPTH, V)), packed)
        int_all[occ, b] = packed
        return carry

    lax.fori_loop(0, 8, pack, 0)
    z_start(0, 0)
    z_start(0, 1)
    pair_start(0)
    pair_start(1)
    unpack((0, 0))
    z_forward(0, 1, 0)
    x_forward(0, 0)
    z_forward(0, 1, 1)
    z_forward(0, 2, 0)
    x_forward(1, 0)
    y_forward(0)
    y_start(1)
    z_forward(0, 2, 1)
    x_end(0, 0)
    pair_end(0)
    z_forward(0, 3, 0)
    pair_end(1)
    z_forward(0, 3, 1)
    x_forward(0, -1)
    z_forward(1, 1, 0)
    y_end(0)
    z_forward(1, 1, 1)
    z_end(0, 0)
    z_end(0, 1)
    unpack((1, 0), (-1, 0), (2, 0), (-2, 0))
    x_forward(0, 1)
    z_forward(1, 2, 0)
    unpack((3, 0), (-3, 0), (4, 0), (0, 1))
    z_forward(1, 2, 1)
    y_forward(1)
    z_forward(1, 3, 0)
    x_forward(0, 2)
    z_forward(1, 3, 1)
    unpack((1, 1), (-1, 1), (2, 1), (-2, 1))
    x_end(0, -1)
    x_end(0, 1)
    unpack((3, 1), (-3, 1))
    z_end(1, 0)
    z_end(1, 1)
    unpack((4, 1))
    contract(0, 0, True)
    y_end(1)
    x_end(0, 2)
    contract(0, 1)
    x_forward(1, -1)
    contract(0, -1)
    contract(0, 2)
    x_forward(1, 1)
    exchange(0)
    x_forward(1, 2)
    x_end(1, 0)
    contract(1, 0, True)
    x_end(1, -1)
    contract(1, 1)
    x_end(1, 1)
    contract(1, -1)
    contract(1, 2, first=-1, count=3)
    x_end(1, 2)
    contract(1, 2, first=2, count=1)
    exchange(1)
    for copy in sent:
        copy.wait_send()
    for copy, arrival in passed:
        arrival.wait_recv()
    for i in range(2):
        for b in range(8):
            for h in range(2):
                out_ref[i, b, :, h * 128 : (h + 1) * 128] = (
                    acc[i, b * NO : (b + 1) * NO, h * 128 : (h + 1) * 128] - mirror[h, pl.ds(i * 8 + b, NO, stride=16), :]
                )
    for copy, arrival in passed:
        copy.wait_send()


MOVES = 2 * (4 + 16 + 16) + 17


def dense(amplitudes, flat_int, mask, tile_irrep):
    vmem = pl.BlockSpec(memory_space=pltpu.VMEM)
    return pl.pallas_call(
        dense_kernel,
        out_shape=jax.ShapeDtypeStruct((2, 8, NO, V), F32),
        in_specs=[vmem, vmem, vmem, pl.BlockSpec(memory_space=pltpu.SMEM)],
        out_specs=vmem,
        scratch_shapes=[
            pltpu.VMEM((2, 32, KW, 8, V), F32),
            pltpu.VMEM((16, V, V), F32),
            pltpu.VMEM((2, V, V), F32),
            pltpu.VMEM((2, 2, V, 128), F32),
            pltpu.VMEM((2, 2 * V, 128), F32),
            pltpu.SemaphoreType.DMA((MOVES,)),
            pltpu.SemaphoreType.DMA((MOVES,)),
            pltpu.SemaphoreType.DMA((30,)),
            pltpu.SemaphoreType.DMA((30,)),
        ],
        compiler_params=pltpu.CompilerParams(collective_id=0, has_side_effects=True, vmem_limit_bytes=48 << 20),
    )(amplitudes, flat_int, mask, tile_irrep)


def sparse(amplitudes, flat_int, mask, tile_irrep):
    vmem = pl.BlockSpec(memory_space=pltpu.VMEM)
    hbm = pl.BlockSpec(memory_space=pl.ANY)
    return pl.pallas_call(
        sparse_kernel,
        out_shape=jax.ShapeDtypeStruct((2, 8, NO, V), F32),
        in_specs=[hbm, hbm, vmem, pl.BlockSpec(memory_space=pltpu.SMEM)],
        out_specs=vmem,
        scratch_shapes=[
            pltpu.VMEM((2, KW, 8, V), F32),
            pltpu.VMEM((KW * 16 * 8, NO), F32),
            pltpu.VMEM((8, NO, V), F32),
            pltpu.VMEM((4, NO, V), jnp.int32),
            pltpu.VMEM((2, 32, KW, 8, V), F32),
            pltpu.VMEM((16, 8, DEPTH, V), F32),
            pltpu.VMEM((16, V, V), BF16),
            pltpu.VMEM((16, V, V), BF16),
            pltpu.VMEM((V, V), F32),
            pltpu.VMEM((2, V, V), F32),
            pltpu.VMEM((2, 2, V, 128), F32),
            pltpu.VMEM((2, 2 * V, 128), F32),
            pltpu.SemaphoreType.DMA((2,)),
            pltpu.SemaphoreType.DMA((MOVES + 13,)),
            pltpu.SemaphoreType.DMA((MOVES + 13,)),
            pltpu.SemaphoreType.DMA((30,)),
            pltpu.SemaphoreType.DMA((30,)),
        ],
        compiler_params=pltpu.CompilerParams(collective_id=1, has_side_effects=True, vmem_limit_bytes=56 << 20),
    )(amplitudes, flat_int, mask, tile_irrep)


def body(amplitudes, integrals, tile_mask, tile_irrep):
    flat_int = integrals.transpose(0, 1, 3, 2).reshape(KW * 16 * 8, NO)
    mask = tile_mask.transpose(0, 2, 3, 1)
    occupied = tile_irrep[:NO]
    pairs = jnp.sum((occupied[:, None] == occupied[None, :]).astype(jnp.int32))
    return lax.cond(pairs < (DEPTH + 1) ** 2, sparse, dense, amplitudes, flat_int, mask, tile_irrep)


def solution(mesh):
    return jax.shard_map(
        body,
        mesh=mesh,
        in_specs=(
            P("occ", None, "vir", None),
            P(None, "occ", None, "vir"),
            P("occ", None, None, None),
            P(),
        ),
        out_specs=P("occ", "vir", None, None),
        check_vma=False,
    )
```

```python
import jax
import jax.numpy as jnp
from jax import lax
from jax.experimental import pallas as pl
from jax.experimental.pallas import tpu as pltpu
from jax.sharding import PartitionSpec as P

NO = 32
V = 256
TILE = 64
KW = 16
DEPTH = 16
FAR_FIRST = (8, 7, 9, 6, 10, 5, 11, 4, 12, 3, 13, 2, 14, 1, 15)
MESH = pl.DeviceIdType.MESH
F32 = jnp.float32
BF16 = jnp.bfloat16


def split(value):
    high = value.astype(BF16)
    return high, (value - high.astype(F32)).astype(BF16)


def dense_kernel(amp_ref, int_ref, mask_ref, irrep_ref, out_ref, amp_all, int_all, acc, cyc, mirror, send_sem, recv_sem, pass_send, pass_recv):
    occ, vir = lax.axis_index("occ"), lax.axis_index("vir")
    z, yl = occ // 2, occ % 2
    x, yh, core = vir // 8, (vir // 2) % 4, vir % 2

    def occ_at(dz, flip):
        return ((z + dz + 8) % 8) * 2 + (yl + flip) % 2

    def vir_at(dx, dy, flip):
        return (((x + dx + 4) % 4) * 4 + (yh + dy + 4) % 4) * 2 + (core + flip) % 2

    barrier = pltpu.get_barrier_semaphore()
    for step in range(1, 16):
        pl.semaphore_signal(barrier, inc=1, device_id=((occ + step) % 16, vir), device_id_type=MESH)
    for dx, dy, flip in ((1, 0, 0), (-1, 0, 0), (0, 1, 0), (0, -1, 0), (0, 0, 1)):
        pl.semaphore_signal(barrier, inc=1, device_id=(occ, vir_at(dx, dy, flip)), device_id_type=MESH)

    spread = (lax.broadcasted_iota(jnp.int32, (4, V), 1) // TILE == lax.broadcasted_iota(jnp.int32, (4, V), 0)).astype(F32)
    for i in range(2):
        kept = lax.dot_general(
            mask_ref[i, vir // 8].astype(F32), spread, (((0,), (0,)), ((), ())), preferred_element_type=F32
        )
        amp_all[i, vir] = amp_ref[i] * kept[:, None, :]

    lane = lax.broadcasted_iota(jnp.int32, (NO, V), 1) // 16
    row = lax.broadcasted_iota(jnp.int32, (NO, V), 0)
    label = jnp.full((NO, V), irrep_ref[NO + occ // 4] ^ irrep_ref[NO + vir // 8], jnp.int32)
    lanes = jnp.zeros((NO, V), jnp.int32)
    rows = jnp.zeros((NO, V), jnp.int32)
    for k in range(KW):
        lanes = jnp.where(lane == k, irrep_ref[k], lanes)
    for j in range(NO):
        rows = jnp.where(row == j, irrep_ref[j], rows)
    symmetry = ((label ^ lanes ^ rows) == 0).astype(F32)
    for b in range(8):
        int_all[occ, b * NO : (b + 1) * NO, :] = int_ref[pl.ds(b, V, stride=8), :].T * symmetry

    pl.semaphore_wait(barrier, 20)

    count = [0]
    sent = []

    def move(source, to, landing):
        slot = count[0]
        count[0] += 1
        copy = pltpu.make_async_remote_copy(
            src_ref=source, dst_ref=source, send_sem=send_sem.at[slot], recv_sem=recv_sem.at[slot], device_id=to, device_id_type=MESH
        )
        copy.start()
        sent.append(copy)
        arrival = pltpu.make_async_remote_copy(
            src_ref=landing, dst_ref=landing, send_sem=send_sem.at[slot], recv_sem=recv_sem.at[slot], device_id=to, device_id_type=MESH
        )
        return arrival.wait_recv

    arrivals = []
    x_wait = {}
    y_wait = {}
    z_wait = {}

    def block(i, dx, dy, flip=0):
        return amp_all.at[i, vir_at(dx, dy, flip)]

    def half(i, dx, dy, upper):
        return amp_all.at[i, vir_at(dx, dy, 0), pl.ds(8 * upper, 8)]

    right, left = (occ, vir_at(1, 0, 0)), (occ, vir_at(-1, 0, 0))
    up, down = (occ, vir_at(0, 1, 0)), (occ, vir_at(0, -1, 0))
    sibling = (occ, vir_at(0, 0, 1))

    def share(i, dx, dy):
        arrivals.append(move(block(i, dx, dy), sibling, block(i, dx, dy, 1)))

    def x_start(i, dy):
        x_wait[i, dy] = (
            move(block(i, 0, dy), right, block(i, -1, dy)),
            move(block(i, 0, dy), left, block(i, 1, dy)),
        )
        share(i, 0, dy)

    def x_forward(i, dy):
        first, second = x_wait[i, dy]
        first()
        one = move(half(i, -1, dy, 0), right, half(i, 2, dy, 0))
        share(i, -1, dy)
        second()
        two = move(half(i, 1, dy, 1), left, half(i, 2, dy, 1))
        share(i, 1, dy)
        x_wait[i, dy] = (one, two)

    def x_end(i, dy):
        one, two = x_wait[i, dy]
        one()
        two()
        share(i, 2, dy)

    def y_start(i):
        y_wait[i] = [move(block(i, 0, 0), up, block(i, 0, -1)), move(block(i, 0, 0), down, block(i, 0, 1))]

    def y_forward(i):
        first, second = y_wait[i]
        first()
        one = move(half(i, 0, -1, 0), up, half(i, 0, 2, 0))
        x_start(i, -1)
        second()
        two = move(half(i, 0, 1, 1), down, half(i, 0, 2, 1))
        x_start(i, 1)
        y_wait[i] = [one, two]

    def y_end(i):
        one, two = y_wait[i]
        one()
        two()
        x_start(i, 2)

    above, below = (occ_at(1, 0), vir), (occ_at(-1, 0), vir)

    def z_start(flip):
        z_wait[flip] = (
            move(int_all.at[occ_at(0, flip)], above, int_all.at[occ_at(-1, flip)]),
            move(int_all.at[occ_at(0, flip)], below, int_all.at[occ_at(1, flip)]),
        )

    def z_forward(flip, hop):
        first, second = z_wait[flip]
        first()
        if hop < 3:
            one = move(int_all.at[occ_at(-hop, flip)], above, int_all.at[occ_at(-hop - 1, flip)])
        else:
            one = move(int_all.at[occ_at(-3, flip), pl.ds(0, 128)], above, int_all.at[occ_at(4, flip), pl.ds(0, 128)])
        second()
        if hop < 3:
            two = move(int_all.at[occ_at(hop, flip)], below, int_all.at[occ_at(hop + 1, flip)])
        else:
            two = move(int_all.at[occ_at(3, flip), pl.ds(128, 128)], below, int_all.at[occ_at(4, flip), pl.ds(128, 128)])
        z_wait[flip] = (one, two)

    def z_end(flip):
        one, two = z_wait[flip]
        one()
        two()

    pair_wait = move(int_all.at[occ], (occ_at(0, 1), vir), int_all.at[occ_at(0, 1)])
    z_start(0)
    y_start(0)
    x_start(0, 0)
    y_start(1)
    x_start(1, 0)
    x_forward(0, 0)
    pair_wait()
    z_start(1)
    z_forward(0, 1)
    y_forward(0)
    x_forward(1, 0)
    y_forward(1)
    z_forward(1, 1)
    x_forward(0, -1)
    x_forward(0, 1)
    y_end(0)
    z_forward(0, 2)
    x_end(0, 0)
    x_end(1, 0)
    y_end(1)
    x_forward(1, -1)
    z_forward(1, 2)
    x_forward(1, 1)
    x_forward(0, 2)
    z_forward(0, 3)
    x_forward(1, 2)
    x_end(0, -1)
    x_end(0, 1)
    x_end(1, -1)
    x_end(1, 1)
    z_forward(1, 3)
    x_end(0, 2)
    x_end(1, 2)
    z_end(0)
    z_end(1)
    for wait in arrivals:
        wait()

    acc[...] = jnp.zeros_like(acc)

    def contract(o, carry):
        int_high, int_low = split(int_all[o])
        left_side = jnp.concatenate([int_high, int_high, int_low], axis=1)
        for i in range(2):
            piece = jnp.concatenate([amp_all[i, 2 * o][:, None], amp_all[i, 2 * o + 1][:, None]], axis=1).reshape(V, V)
            amp_high, amp_low = split(piece)
            right_side = jnp.concatenate([amp_high, amp_low, amp_high], axis=0)
            acc[i] += jnp.dot(left_side, right_side, preferred_element_type=F32)
        return carry

    lax.fori_loop(0, 16, contract, 0)

    for i in range(2):
        for b in range(8):
            for h in range(2):
                cyc[i, h, pl.ds(b, NO, stride=8), :] = acc[i, b * NO : (b + 1) * NO, h * 128 : (h + 1) * 128]
    passed = []
    for i in range(2):
        for step in range(1, 16):
            slot = i * 15 + step - 1
            to, origin = (occ + step) % 16, (occ + 16 - step) % 16
            copy = pltpu.make_async_remote_copy(
                src_ref=cyc.at[i, :, pl.ds(16 * to, 16)],
                dst_ref=mirror.at[:, pl.ds((2 * occ + i) * 16, 16)],
                send_sem=pass_send.at[slot],
                recv_sem=pass_recv.at[slot],
                device_id=(to, vir),
                device_id_type=MESH,
            )
            copy.start()
            landing = mirror.at[:, pl.ds((2 * origin + i) * 16, 16)]
            passed.append(
                (
                    copy,
                    pltpu.make_async_remote_copy(
                        src_ref=landing,
                        dst_ref=landing,
                        send_sem=pass_send.at[slot],
                        recv_sem=pass_recv.at[slot],
                        device_id=(to, vir),
                        device_id_type=MESH,
                    ),
                )
            )
        mirror[:, pl.ds((2 * occ + i) * 16, 16), :] = cyc[i, :, pl.ds(16 * occ, 16), :]
    for copy, arrival in passed:
        arrival.wait_recv()
    for i in range(2):
        for b in range(8):
            for h in range(2):
                out_ref[i, b, :, h * 128 : (h + 1) * 128] = (
                    acc[i, b * NO : (b + 1) * NO, h * 128 : (h + 1) * 128] - mirror[h, pl.ds(i * 8 + b, NO, stride=16), :]
                )
    for copy in sent:
        copy.wait_send()
    for copy, arrival in passed:
        copy.wait_send()


def sparse_kernel(
    amp_hbm, int_hbm, mask_ref, irrep_ref, out_ref,
    amp_in, int_in, turned, slots, amp_all, int_all, high_all, low_all, wide, acc, cyc, mirror,
    in_sem, send_sem, recv_sem, pass_send, pass_recv,
):
    occ, vir = lax.axis_index("occ"), lax.axis_index("vir")
    z, yl = occ // 2, occ % 2
    x, yh, core = vir // 8, (vir // 2) % 4, vir % 2

    def occ_at(dz, flip):
        return ((z + dz + 8) % 8) * 2 + (yl + flip) % 2

    def vir_at(dx, dy, flip):
        return (((x + dx + 4) % 4) * 4 + (yh + dy + 4) % 4) * 2 + (core + flip) % 2

    barrier = pltpu.get_barrier_semaphore()
    for step in range(1, 16):
        pl.semaphore_signal(barrier, inc=1, device_id=((occ + step) % 16, vir), device_id_type=MESH)
    for dx, dy, flip in ((1, 0, 0), (-1, 0, 0), (0, 1, 0), (0, -1, 0), (0, 0, 1)):
        pl.semaphore_signal(barrier, inc=1, device_id=(occ, vir_at(dx, dy, flip)), device_id_type=MESH)
    load_int = pltpu.make_async_copy(int_hbm, int_in, in_sem.at[0])
    load_amp = pltpu.make_async_copy(amp_hbm, amp_in, in_sem.at[1])
    load_amp.start()
    load_int.start()

    spread = (lax.broadcasted_iota(jnp.int32, (4, V), 1) // TILE == lax.broadcasted_iota(jnp.int32, (4, V), 0)).astype(F32)
    load_amp.wait()
    def mask(i):
        kept = lax.dot_general(
            mask_ref[i, vir // 8].astype(F32), spread, (((0,), (0,)), ((), ())), preferred_element_type=F32
        )
        amp_all[i, vir] = amp_in[i] * kept[:, None, :]

    mask(0)
    pl.semaphore_wait(barrier, 20)

    count = [0]
    sent = []

    def move(source, to, landing):
        slot = count[0]
        count[0] += 1
        copy = pltpu.make_async_remote_copy(
            src_ref=source, dst_ref=source, send_sem=send_sem.at[slot], recv_sem=recv_sem.at[slot], device_id=to, device_id_type=MESH
        )
        copy.start()
        sent.append(copy)
        arrival = pltpu.make_async_remote_copy(
            src_ref=landing, dst_ref=landing, send_sem=send_sem.at[slot], recv_sem=recv_sem.at[slot], device_id=to, device_id_type=MESH
        )
        return arrival.wait_recv

    share_wait = {}
    x_wait = {}
    y_wait = {}
    z_wait = {}

    def block(i, dx, dy, flip=0):
        return amp_all.at[i, vir_at(dx, dy, flip)]

    def half(i, dx, dy, upper):
        return amp_all.at[i, vir_at(dx, dy, 0), pl.ds(8 * upper, 8)]

    right, left = (occ, vir_at(1, 0, 0)), (occ, vir_at(-1, 0, 0))
    up, down = (occ, vir_at(0, 1, 0)), (occ, vir_at(0, -1, 0))
    sibling = (occ, vir_at(0, 0, 1))

    def share(i, dx, dy):
        share_wait[i, dx, dy] = move(block(i, dx, dy), sibling, block(i, dx, dy, 1))

    def x_start(i, dy):
        x_wait[i, dy] = (
            move(block(i, 0, dy), right, block(i, -1, dy)),
            move(block(i, 0, dy), left, block(i, 1, dy)),
        )
        share(i, 0, dy)

    def x_forward(i, dy):
        first, second = x_wait[i, dy]
        first()
        one = move(half(i, -1, dy, 0), right, half(i, 2, dy, 0))
        share(i, -1, dy)
        second()
        two = move(half(i, 1, dy, 1), left, half(i, 2, dy, 1))
        share(i, 1, dy)
        x_wait[i, dy] = (one, two)

    def x_end(i, dy):
        one, two = x_wait[i, dy]
        one()
        two()
        share(i, 2, dy)

    def y_start(i):
        y_wait[i] = [move(block(i, 0, 0), up, block(i, 0, -1)), move(block(i, 0, 0), down, block(i, 0, 1))]

    def y_forward(i):
        first, second = y_wait[i]
        first()
        one = move(half(i, 0, -1, 0), up, half(i, 0, 2, 0))
        x_start(i, -1)
        second()
        two = move(half(i, 0, 1, 1), down, half(i, 0, 2, 1))
        x_start(i, 1)
        y_wait[i] = [one, two]

    def y_end(i):
        one, two = y_wait[i]
        one()
        two()
        x_start(i, 2)

    above, below_z = (occ_at(1, 0), vir), (occ_at(-1, 0), vir)

    def piece(dz, flip, part):
        return int_all.at[occ_at(dz, flip), pl.ds(4 * part, 4)]

    def z_start(flip, part):
        z_wait[flip, part] = [
            move(piece(0, flip, part), above, piece(-1, flip, part)),
            move(piece(0, flip, part), below_z, piece(1, flip, part)),
        ]

    def z_forward(flip, hop, part):
        first, second = z_wait[flip, part]
        onward = []
        first()
        if hop < 3 or part == 0:
            onward.append(move(piece(-hop, flip, part), above, piece(-hop - 1, flip, part)))
        second()
        if hop < 3 or part == 1:
            onward.append(move(piece(hop, flip, part), below_z, piece(hop + 1, flip, part)))
        z_wait[flip, part] = onward

    def z_end(flip, part):
        for wait in z_wait[flip, part]:
            wait()

    def pair_start(part):
        z_wait["pair", part] = move(piece(0, 0, part), (occ_at(0, 1), vir), piece(0, 1, part))

    def pair_end(part):
        z_wait["pair", part]()
        z_start(1, part)

    def unpack(*places):
        for dz, flip in places:
            o = occ_at(dz, flip)

            def one(b, carry, o=o):
                for g in range(4):
                    for h in range(2):
                        cols = pl.ds(128 * h, 128)
                        place = slots[o // 4, 8 * g : 8 * g + 8, cols]
                        near = jnp.take_along_axis(int_all[o, b, 0:8, cols], place & 7, axis=0)
                        far = jnp.take_along_axis(int_all[o, b, 8:16, cols], place & 7, axis=0)
                        value = jnp.where(place < 0, 0.0, jnp.where(place < 8, near, far))
                        wide[pl.ds(b * NO + 8 * g, 8), cols] = value
                return carry

            lax.fori_loop(0, 8, one, 0)
            high_all[o], low_all[o] = split(wide[...])

    def contract(i, dx, start=False, first=-1, count=4):
        base = ((x + dx + 4) % 4) * 4

        def one(step, carry):
            o = base + (yh + first + step + 4) % 4
            high = high_all[o]
            left_side = jnp.concatenate([high, high, low_all[o]], axis=1)
            piece = jnp.concatenate([amp_all[i, 2 * o][:, None], amp_all[i, 2 * o + 1][:, None]], axis=1).reshape(V, V)
            amp_high, amp_low = split(piece)
            right_side = jnp.concatenate([amp_high, amp_low, amp_high], axis=0)
            acc[i] += jnp.dot(left_side, right_side, preferred_element_type=F32)
            return carry

        for dy in range(first, first + count):
            share_wait[i, dx, dy]()
        if start:
            acc[i] = jnp.zeros((V, V), F32)
        lax.fori_loop(0, count, one, 0)

    passed = []

    def exchange(i):
        for b in range(8):
            for h in range(2):
                cyc[i, h, pl.ds(b, NO, stride=8), :] = acc[i, b * NO : (b + 1) * NO, h * 128 : (h + 1) * 128]
        for step in FAR_FIRST:
            slot = i * 15 + step - 1
            to, origin = (occ + step) % 16, (occ + 16 - step) % 16
            copy = pltpu.make_async_remote_copy(
                src_ref=cyc.at[i, :, pl.ds(16 * to, 16)],
                dst_ref=mirror.at[:, pl.ds((2 * occ + i) * 16, 16)],
                send_sem=pass_send.at[slot],
                recv_sem=pass_recv.at[slot],
                device_id=(to, vir),
                device_id_type=MESH,
            )
            copy.start()
            landing = mirror.at[:, pl.ds((2 * origin + i) * 16, 16)]
            arrival = pltpu.make_async_remote_copy(
                src_ref=landing,
                dst_ref=landing,
                send_sem=pass_send.at[slot],
                recv_sem=pass_recv.at[slot],
                device_id=(to, vir),
                device_id_type=MESH,
            )
            passed.append((copy, arrival))
        mirror[:, pl.ds((2 * occ + i) * 16, 16), :] = cyc[i, :, pl.ds(16 * occ, 16), :]

    y_start(0)
    x_start(0, 0)
    mask(1)
    x_start(1, 0)

    lane = lax.broadcasted_iota(jnp.int32, (NO, V), 1) // 16
    row = lax.broadcasted_iota(jnp.int32, (NO, V), 0)
    labels = jnp.full((NO, V), irrep_ref[NO + vir // 8], jnp.int32)
    for k in range(KW):
        labels = jnp.where(lane == k, labels ^ irrep_ref[k], labels)
    for j in range(NO):
        labels = jnp.where(row == j, labels ^ irrep_ref[j], labels)
    below = (lax.broadcasted_iota(jnp.int32, (NO, NO), 1) < lax.broadcasted_iota(jnp.int32, (NO, NO), 0)).astype(F32)
    for tile in range(4):
        allowed = (labels ^ irrep_ref[NO + tile]) == 0
        rank = jnp.dot(below, allowed.astype(F32), preferred_element_type=F32)
        slots[tile] = jnp.where(allowed, rank.astype(jnp.int32), -1)

    load_int.wait()
    for b in range(8):
        turned[b] = int_in[pl.ds(b, V, stride=8), :].T
    depth = lax.broadcasted_iota(jnp.int32, (DEPTH, V), 0)

    def pack(b, carry):
        packed = jnp.zeros((DEPTH, V), F32)
        for j in range(NO):
            place = jnp.broadcast_to(slots[occ // 4, j : j + 1, :], (DEPTH, V))
            packed = jnp.where(place == depth, jnp.broadcast_to(turned[b, j : j + 1, :], (DEPTH, V)), packed)
        int_all[occ, b] = packed
        return carry

    lax.fori_loop(0, 8, pack, 0)
    z_start(0, 0)
    z_start(0, 1)
    pair_start(0)
    pair_start(1)
    unpack((0, 0))
    z_forward(0, 1, 0)
    x_forward(0, 0)
    z_forward(0, 1, 1)
    z_forward(0, 2, 0)
    x_forward(1, 0)
    y_forward(0)
    y_start(1)
    z_forward(0, 2, 1)
    x_end(0, 0)
    pair_end(0)
    z_forward(0, 3, 0)
    pair_end(1)
    z_forward(0, 3, 1)
    x_forward(0, -1)
    z_forward(1, 1, 0)
    y_end(0)
    z_forward(1, 1, 1)
    z_end(0, 0)
    z_end(0, 1)
    unpack((1, 0), (-1, 0), (2, 0), (-2, 0))
    x_forward(0, 1)
    z_forward(1, 2, 0)
    unpack((3, 0), (-3, 0), (4, 0), (0, 1))
    z_forward(1, 2, 1)
    y_forward(1)
    z_forward(1, 3, 0)
    x_forward(0, 2)
    z_forward(1, 3, 1)
    unpack((1, 1), (-1, 1), (2, 1), (-2, 1))
    x_end(0, -1)
    x_end(0, 1)
    unpack((3, 1), (-3, 1))
    z_end(1, 0)
    z_end(1, 1)
    unpack((4, 1))
    contract(0, 0, True)
    y_end(1)
    x_end(0, 2)
    contract(0, 1)
    x_forward(1, -1)
    contract(0, -1)
    contract(0, 2)
    x_forward(1, 1)
    exchange(0)
    x_forward(1, 2)
    x_end(1, 0)
    contract(1, 0, True)
    x_end(1, -1)
    contract(1, 1)
    x_end(1, 1)
    contract(1, -1)
    contract(1, 2, first=-1, count=3)
    x_end(1, 2)
    contract(1, 2, first=2, count=1)
    exchange(1)
    for copy in sent:
        copy.wait_send()
    for copy, arrival in passed:
        arrival.wait_recv()
    for i in range(2):
        for b in range(8):
            for h in range(2):
                out_ref[i, b, :, h * 128 : (h + 1) * 128] = (
                    acc[i, b * NO : (b + 1) * NO, h * 128 : (h + 1) * 128] - mirror[h, pl.ds(i * 8 + b, NO, stride=16), :]
                )
    for copy, arrival in passed:
        copy.wait_send()


MOVES = 2 * (4 + 16 + 16) + 17


def dense(amplitudes, flat_int, mask, tile_irrep):
    vmem = pl.BlockSpec(memory_space=pltpu.VMEM)
    return pl.pallas_call(
        dense_kernel,
        out_shape=jax.ShapeDtypeStruct((2, 8, NO, V), F32),
        in_specs=[vmem, vmem, vmem, pl.BlockSpec(memory_space=pltpu.SMEM)],
        out_specs=vmem,
        scratch_shapes=[
            pltpu.VMEM((2, 32, KW, 8, V), F32),
            pltpu.VMEM((16, V, V), F32),
            pltpu.VMEM((2, V, V), F32),
            pltpu.VMEM((2, 2, V, 128), F32),
            pltpu.VMEM((2, 2 * V, 128), F32),
            pltpu.SemaphoreType.DMA((MOVES,)),
            pltpu.SemaphoreType.DMA((MOVES,)),
            pltpu.SemaphoreType.DMA((30,)),
            pltpu.SemaphoreType.DMA((30,)),
        ],
        compiler_params=pltpu.CompilerParams(collective_id=0, has_side_effects=True, vmem_limit_bytes=48 << 20),
    )(amplitudes, flat_int, mask, tile_irrep)


def sparse(amplitudes, flat_int, mask, tile_irrep):
    vmem = pl.BlockSpec(memory_space=pltpu.VMEM)
    hbm = pl.BlockSpec(memory_space=pl.ANY)
    return pl.pallas_call(
        sparse_kernel,
        out_shape=jax.ShapeDtypeStruct((2, 8, NO, V), F32),
        in_specs=[hbm, hbm, vmem, pl.BlockSpec(memory_space=pltpu.SMEM)],
        out_specs=vmem,
        scratch_shapes=[
            pltpu.VMEM((2, KW, 8, V), F32),
            pltpu.VMEM((KW * 16 * 8, NO), F32),
            pltpu.VMEM((8, NO, V), F32),
            pltpu.VMEM((4, NO, V), jnp.int32),
            pltpu.VMEM((2, 32, KW, 8, V), F32),
            pltpu.VMEM((16, 8, DEPTH, V), F32),
            pltpu.VMEM((16, V, V), BF16),
            pltpu.VMEM((16, V, V), BF16),
            pltpu.VMEM((V, V), F32),
            pltpu.VMEM((2, V, V), F32),
            pltpu.VMEM((2, 2, V, 128), F32),
            pltpu.VMEM((2, 2 * V, 128), F32),
            pltpu.SemaphoreType.DMA((2,)),
            pltpu.SemaphoreType.DMA((MOVES + 13,)),
            pltpu.SemaphoreType.DMA((MOVES + 13,)),
            pltpu.SemaphoreType.DMA((30,)),
            pltpu.SemaphoreType.DMA((30,)),
        ],
        compiler_params=pltpu.CompilerParams(collective_id=1, has_side_effects=True, vmem_limit_bytes=56 << 20),
    )(amplitudes, flat_int, mask, tile_irrep)


def body(amplitudes, integrals, tile_mask, tile_irrep):
    flat_int = integrals.transpose(0, 1, 3, 2).reshape(KW * 16 * 8, NO)
    mask = tile_mask.transpose(0, 2, 3, 1)
    occupied = tile_irrep[:NO]
    pairs = jnp.sum((occupied[:, None] == occupied[None, :]).astype(jnp.int32))
    return lax.cond(pairs < (DEPTH + 1) ** 2, sparse, dense, amplitudes, flat_int, mask, tile_irrep)


def solution(mesh):
    return jax.shard_map(
        body,
        mesh=mesh,
        in_specs=(
            P("occ", None, "vir", None),
            P(None, "occ", None, "vir"),
            P("occ", None, None, None),
            P(),
        ),
        out_specs=P("occ", "vir", None, None),
        check_vma=False,
    )
```
